256 devices in a mesh: grp: 2 (over z_hi), dp: 16 (over y, z_lo), row: 8 (over x, core).
Axes of the slice: x: 4, y: 4, z: 8 (z_hi: 2, z_lo: 4; z = z_hi * 4 + z_lo), core: 2. Of those that a mesh axis runs over, the one named last changes fastest.
Arguments:
- images: bfloat16 [2, 16, 64, 256, 256], P('grp', 'dp', 'row'), may hold values from -28 to 28
- w_in: bfloat16 [2, 256, 1024], P('grp', 'dp'), may hold values from -0.375 to 0.375
- w_out: bfloat16 [2, 1024, 256], P('grp', 'dp'), may hold values from -0.1875 to 0.1875
- kernel: bfloat16 [2, 7, 7, 256], P('grp'), may hold values from -0.875 to 0.875
- gain: bfloat16 [2, 256], P('grp'), may hold values from 0.099609375 to 1.8984375
- scale: bfloat16 [2, 256], P('grp'), may hold values from 0.19921875 to 1
Outputs:
- features: bfloat16 [2, 16, 64, 256, 256], P('grp', 'dp', 'row')
- grad_w_in: float32 [2, 256, 1024], P('grp', 'dp')
- grad_w_out: float32 [2, 1024, 256], P('grp', 'dp')
- grad_kernel: float32 [2, 7, 7, 256], P('grp')
- grad_gain: float32 [2, 256], P('grp')
- grad_scale: float32 [2, 256], P('grp')
The draws below stay inside these ranges and needn't reach their ends.
All inputs are finite; a program needn't handle non-finite values.
Results may differ from the reference program's by a relative error of at most 0.012.
Values may be sent and summed in bfloat16 or wider, within the bound.
No kernel may reach another device: no remote copies, remote signals or barrier semaphores. Data moves between devices by JAX's collectives and lax.ppermute only.
A program may use at most 128 MiB of HBM per device.

```python
import math
import jax
import jax.numpy as jnp
from jax import lax

C = 256
HID = 1024
KERNEL = 7
WIDTH_PIX = 256
GROUPS = 2
IMAGES = 16
HEIGHT = 64


def draw_images(key, part):
    key_base, key_amp, key_tilt = jax.random.split(key, 3)
    full_shape = (GROUPS, IMAGES, HEIGHT, WIDTH_PIX, C)
    small_shape = (GROUPS, IMAGES, 1, 1, C)
    base_noise = jax.random.truncated_normal(key_base, -6.0, 6.0, full_shape, jnp.float32)
    amplitude = jnp.exp(jax.random.uniform(key_amp, small_shape, jnp.float32, math.log(0.15), math.log(1.5)))
    tilt_rate = jax.random.uniform(key_tilt, small_shape, jnp.float32, -1.1, 1.1)
    height_pos = (jnp.arange(HEIGHT, dtype=jnp.float32) * (2.0 / (HEIGHT - 1)) - 1.0).reshape(1, 1, HEIGHT, 1, 1)
    return (base_noise * amplitude * jnp.exp(tilt_rate * height_pos)).astype(jnp.bfloat16)


def levels(rng, extent, cuts, least, top_value):
    level = 1.0
    for dim, shards_of in cuts:
        steps = jax.random.uniform(jax.random.fold_in(jax.random.fold_in(rng, 6), dim), (shards_of,), jnp.float32, least / len(cuts), top_value / len(cuts))
        level = level * jnp.repeat(jnp.exp(steps), extent[dim] // shards_of).reshape((-1,) + (1,) * (len(extent) - 1 - dim))
    return level


def scatter_about(stream_key, shape, width, reach, cuts=(), held_as=jnp.bfloat16):
    array = jax.random.normal(stream_key, shape, jnp.float32) * width
    if len(cuts) > 0:
        array = levels(stream_key, shape, cuts, -0.22, 0.18) * array
    return jnp.clip(array, min=-reach, max=reach).astype(held_as)


def setup_inputs(seed: int = 0) -> dict:
    key_list = jax.random.split(jax.random.key(seed), 7)
    return {
        "images": draw_images(jax.random.fold_in(key_list[6], 71), 0),
        "w_in": scatter_about(key_list[1], (GROUPS, C, HID), C ** -0.5, 0.375, ((0, 2), (1, 16))),
        "w_out": scatter_about(key_list[2], (GROUPS, HID, C), HID ** -0.5, 0.1875, ((0, 2), (1, 16))),
        "kernel": scatter_about(key_list[3], (GROUPS, KERNEL, KERNEL, C), (KERNEL * KERNEL) ** -0.5, 0.875, ((0, 2),)),
        "gain": jnp.clip(1.0 + 0.18 * jax.random.normal(key_list[4], (GROUPS, C), jnp.float32), 0.099609375, 1.8984375).astype(jnp.bfloat16),
        "scale": jnp.clip(jnp.exp(math.log(1.0) - 1.6133518 * jax.random.uniform(key_list[5], (GROUPS, C), jnp.float32) ** levels(key_list[5], (GROUPS, C), ((0, 2),), -0.2, 0.2)), 0.19921875, 1.0).astype(jnp.bfloat16),
    }


SQRT_HALF = 0.7071067811865476
INV_SQRT_TAU = 0.3989422804014327

def gelu_exact(values):
    return 0.5 * values * (1.0 + jax.scipy.special.erf(values * SQRT_HALF))

def gelu_slope(values):
    return 0.5 * (1.0 + jax.scipy.special.erf(values * SQRT_HALF)) + values * jnp.exp(-0.5 * values * values) * INV_SQRT_TAU

def depthwise(padded, weights, row_count, col_count):
    summed = jnp.zeros(padded.shape[:-3] + (row_count, col_count, padded.shape[-1]), jnp.float32)
    for tap_row in range(weights.shape[0]):
        for tap_col in range(weights.shape[1]):
            summed = summed + padded[..., tap_row:tap_row + row_count, tap_col:tap_col + col_count, :] * weights[tap_row, tap_col]
    return summed

def kernel_grad(padded, upstream, row_count, col_count, tap_count):
    leading_axes = tuple(range(upstream.ndim - 1))
    tap_terms = []
    for tap_row in range(tap_count):
        for tap_col in range(tap_count):
            window = padded[..., tap_row:tap_row + row_count, tap_col:tap_col + col_count, :]
            tap_terms.append(lax.optimization_barrier(jnp.sum(window * upstream, axis=leading_axes)))
    return jnp.stack(tap_terms).reshape(tap_count, tap_count, -1)

def branch_forward(filtered, gain_vec, weight_in, weight_out):
    channels = filtered.shape[-1]
    flat_conv = filtered.reshape(-1, channels)
    row_mean = lax.optimization_barrier(jnp.mean(flat_conv, axis=-1, keepdims=True))
    centred = flat_conv - row_mean
    inv_std = lax.rsqrt(lax.optimization_barrier(jnp.mean(centred * centred, axis=-1, keepdims=True)) + 1e-06)
    unit_rows = centred * inv_std
    normed = (unit_rows * gain_vec).astype(jnp.bfloat16)
    pre_act = jnp.dot(normed, weight_in, preferred_element_type=jnp.float32)
    activated = gelu_exact(pre_act).astype(jnp.bfloat16)
    branch = jnp.dot(activated, weight_out, preferred_element_type=jnp.float32)
    return (normed, unit_rows, inv_std, pre_act, activated, branch)

def branch_backward(upstream, cache, gain_vec, scale_vec, weight_in, weight_out):
    normed, unit_rows, inv_std, pre_act, activated, branch = cache
    grad_scale = lax.optimization_barrier(jnp.sum(upstream * branch, axis=0))
    up_branch = (upstream * scale_vec).astype(jnp.bfloat16)
    grad_out = jnp.dot(activated.T, up_branch, preferred_element_type=jnp.float32)
    up_active = jnp.dot(up_branch, weight_out.T, preferred_element_type=jnp.float32)
    up_pre = (up_active * gelu_slope(pre_act)).astype(jnp.bfloat16)
    grad_in = jnp.dot(normed.T, up_pre, preferred_element_type=jnp.float32)
    up_normed = jnp.dot(up_pre, weight_in.T, preferred_element_type=jnp.float32)
    grad_gain = lax.optimization_barrier(jnp.sum(up_normed * unit_rows, axis=0))
    up_unit = up_normed * gain_vec
    up_conv = inv_std * (up_unit - lax.optimization_barrier(jnp.mean(up_unit, axis=-1, keepdims=True)) - unit_rows * lax.optimization_barrier(jnp.mean(up_unit * unit_rows, axis=-1, keepdims=True)))
    return (grad_in, grad_out, grad_gain, grad_scale, up_conv)

def reference(images, w_in, w_out, kernel, gain, scale):
    inv_count = 1.0 / (IMAGES * HEIGHT * WIDTH_PIX)
    edge = KERNEL // 2
    feature_list, in_list, out_list, kernel_list, gain_list, scale_list = ([], [], [], [], [], [])
    for group in range(GROUPS):
        mentor = GROUPS - 1 - group
        own_kernel = kernel[group].astype(jnp.float32)
        own_gain = gain[group].astype(jnp.float32)
        own_scale = scale[group].astype(jnp.float32)
        mentor_kernel = kernel[mentor].astype(jnp.float32)
        mentor_gain = gain[mentor].astype(jnp.float32)
        mentor_scale = scale[mentor].astype(jnp.float32)
        own_in, own_out = (w_in[group], w_out[group])
        mentor_in, mentor_out = (w_in[mentor], w_out[mentor])

        def one_image(carry, picture):
            picture_f = picture.astype(jnp.float32)
            padded = jnp.pad(picture_f, ((edge, edge), (edge, edge), (0, 0)))
            own_cache = branch_forward(depthwise(padded, own_kernel, HEIGHT, WIDTH_PIX), own_gain, own_in, own_out)
            mentor_cache = branch_forward(depthwise(padded, mentor_kernel, HEIGHT, WIDTH_PIX), mentor_gain, mentor_in, mentor_out)
            mismatch = own_scale * own_cache[5] - mentor_scale * mentor_cache[5]
            upstream = mismatch * inv_count
            grad_in, grad_out, grad_gain, grad_scale, up_conv = branch_backward(upstream, own_cache, own_gain, own_scale, own_in, own_out)
            grad_kern = kernel_grad(padded, up_conv.reshape(HEIGHT, WIDTH_PIX, -1), HEIGHT, WIDTH_PIX, KERNEL)
            feats = (picture_f + own_scale * own_cache[5].reshape(HEIGHT, WIDTH_PIX, -1)).astype(jnp.bfloat16)
            new_carry = (carry[0] + grad_in, carry[1] + grad_out, carry[2] + grad_kern, carry[3] + grad_gain, carry[4] + grad_scale)
            return (new_carry, feats)
        start = (jnp.zeros((C, HID), jnp.float32), jnp.zeros((HID, C), jnp.float32), jnp.zeros((KERNEL, KERNEL, C), jnp.float32), jnp.zeros((C,), jnp.float32), jnp.zeros((C,), jnp.float32))
        totals, feats = lax.scan(one_image, start, images[group])
        feature_list.append(feats)
        in_list.append(totals[0])
        out_list.append(totals[1])
        kernel_list.append(totals[2])
        gain_list.append(totals[3])
        scale_list.append(totals[4])
    return (jnp.stack(feature_list), jnp.stack(in_list), jnp.stack(out_list), jnp.stack(kernel_list), jnp.stack(gain_list), jnp.stack(scale_list))
```

```python
import functools

import jax
import jax.numpy as jnp
from jax import lax
from jax.experimental import pallas as pl
from jax.experimental.pallas import tpu as pltpu
from jax.sharding import PartitionSpec as P

SQRT_HALF = 0.7071067811865476
INV_SQRT_TAU = 0.3989422804014327
BF = jnp.bfloat16
F32 = jnp.float32
LEFT = 8


def ring(axis, shift, size=None):
    count = lax.axis_size(axis)
    return [(i, (i + shift) % count) for i in range(count)]


def fill_padded(pad, img, top, bot, edge):
    rows, cols, chans = img.shape
    zero = jnp.zeros((8, 128), F32)
    for cb in range(chans // 128):
        lanes = slice(cb * 128, cb * 128 + 128)
        for r in range(rows + 2 * edge):
            if r < edge:
                ref, q = top, r
            elif r < rows + edge:
                ref, q = img, r - edge
            else:
                ref, q = bot, r - rows - edge
            pad[cb, r, 0:LEFT, :] = zero
            pad[cb, r, LEFT + cols : LEFT + cols + 8, :] = zero
            pad[cb, r, LEFT : LEFT + cols, :] = ref[q, :, lanes].astype(F32)


def conv_norm_kernel(
    img, top, bot, k_own, k_men, g_own, g_men, n_own, n_men, unit_o, inv_o, pad, filt, *, taps
):
    rows, cols, chans = img.shape
    edge = taps // 2
    fill_padded(pad, img, top, bot, edge)
    for cb in range(chans // 128):
        lanes = slice(cb * 128, cb * 128 + 128)

        def block(wb, _):
            w0 = pl.multiple_of(wb * 8, 8)
            accs = [[None] * rows, [None] * rows]
            for j in range(taps):
                weights = [
                    [jnp.broadcast_to(k[i * taps + j : i * taps + j + 1, lanes], (8, 128)) for i in range(taps)]
                    for k in (k_own, k_men)
                ]
                for r in range(rows + 2 * edge):
                    v = pad[cb, r, pl.ds(w0 + (LEFT - edge + j), 8), :]
                    for i in range(taps):
                        h = r - i
                        if 0 <= h < rows:
                            for s in range(2):
                                term = v * weights[s][i]
                                accs[s][h] = term if accs[s][h] is None else accs[s][h] + term
            for h in range(rows):
                for s in range(2):
                    filt[s, h, pl.ds(w0, 8), lanes] = accs[s][h]
            return 0

        lax.fori_loop(0, cols // 8, block, 0)
    span = 64
    for s, gain, normed in ((0, g_own, n_own), (1, g_men, n_men)):

        def norm(t, _):
            h = t // (cols // span)
            w0 = pl.multiple_of((t % (cols // span)) * span, span)
            at = pl.multiple_of(t * span, span)
            x = filt[s, h, pl.ds(w0, span), :]
            centred = x - jnp.mean(x, axis=-1, keepdims=True)
            inv = lax.rsqrt(jnp.mean(centred * centred, axis=-1, keepdims=True) + 1e-06)
            unit = centred * inv
            normed[pl.ds(at, span), :] = (unit * gain[...]).astype(BF)
            if s == 0:
                unit_o[pl.ds(at, span), :] = unit
                inv_o[pl.ds(at, span), :] = inv
            return 0

        lax.fori_loop(0, rows * cols // span, norm, 0)


def conv_norm(img, top, bot, k_own, k_men, g_own, g_men, taps):
    rows, cols, chans = img.shape
    edge = taps // 2
    pixels = rows * cols
    return pl.pallas_call(
        functools.partial(conv_norm_kernel, taps=taps),
        out_shape=[
            jax.ShapeDtypeStruct((pixels, chans), BF),
            jax.ShapeDtypeStruct((pixels, chans), BF),
            jax.ShapeDtypeStruct((pixels, chans), F32),
            jax.ShapeDtypeStruct((pixels, 1), F32),
        ],
        scratch_shapes=[
            pltpu.VMEM((chans // 128, rows + 2 * edge, cols + LEFT + 8, 128), F32),
            pltpu.VMEM((2, rows, cols, chans), F32),
        ],
        name="conv_norm",
    )(img, top, bot, k_own, k_men, g_own, g_men)


def pointwise_kernel(place, *refs, nx, inv_count):
    bufs = refs[: 2 * nx]
    (n_own, n_men, unit_i, inv_i, img, gain, s_own, s_men) = refs[2 * nx : 2 * nx + 8]
    (feat, up_conv, parts, gsum) = refs[2 * nx + 8 : 2 * nx + 12]
    (w_in, w_out, act, slope, g_in, g_out) = refs[2 * nx + 12 :]
    step = pl.program_id(0)
    tile, chans = n_own.shape
    hid = w_out.shape[2]
    dp = bufs[0].shape[0]
    chunks = hid // 256
    me_x, me_c = place[0], place[1]
    per_d = hid // dp

    @pl.when(step == 0)
    def _():
        for k in range(nx):
            x = lax.rem(me_x - k + nx, nx)
            for c in range(2):
                h = me_c if c == 0 else 1 - me_c
                buf = bufs[2 * k + c]
                for d in range(dp):
                    for s in range(2):
                        w_in[s, 2 * x + h, d * 16 : d * 16 + 16, :] = buf[d, s * 16 : s * 16 + 16, 0:128]
                        w_out[s, h, pl.ds(pl.multiple_of(d * per_d + x * 16, 16), 16), :] = buf[
                            d, s * 16 : s * 16 + 16, 128:256
                        ]
        g_in[...] = jnp.zeros_like(g_in)
        g_out[...] = jnp.zeros_like(g_out)
        gsum[...] = jnp.zeros_like(gsum)

    def in_chunk(s, n):
        return jnp.concatenate([w_in[s, 2 * n], w_in[s, 2 * n + 1]], axis=1)

    def out_chunk(s, n):
        rows = slice(n * 256, n * 256 + 256)
        return jnp.concatenate([w_out[s, 0, rows, :], w_out[s, 1, rows, :]], axis=1)

    branch = [None, None]
    for s, normed in ((0, n_own), (1, n_men)):
        x = normed[...]
        for n in range(chunks):
            pre = jnp.dot(x, in_chunk(s, n), preferred_element_type=F32)
            half_cdf = 0.5 + 0.5 * lax.erf(pre * SQRT_HALF)
            activated = (pre * half_cdf).astype(BF)
            if s == 0:
                act[:, n * 256 : n * 256 + 256] = activated
                slope[:, n * 256 : n * 256 + 256] = (
                    half_cdf + pre * jnp.exp(-0.5 * pre * pre) * INV_SQRT_TAU
                )
            part = jnp.dot(activated, out_chunk(s, n), preferred_element_type=F32)
            branch[s] = part if branch[s] is None else branch[s] + part
    scaled = branch[0] * s_own[...]
    feat[...] = (img[...].astype(F32) + scaled).astype(BF)
    upstream = (scaled - s_men[...] * branch[1]) * inv_count
    gsum[1:2, :] = gsum[1:2, :] + jnp.sum(upstream * branch[0], axis=0, keepdims=True)
    up_branch = (upstream * s_own[...]).astype(BF)
    up_branch_t = up_branch.T
    normed_t = n_own[...].T
    up_normed = None
    for n in range(chunks):
        cols = slice(n * 256, n * 256 + 256)
        g_out[:, cols] = g_out[:, cols] + jnp.dot(up_branch_t, act[:, cols], preferred_element_type=F32)
        up_active = lax.dot_general(
            up_branch, out_chunk(0, n), (((1,), (1,)), ((), ())), preferred_element_type=F32
        )
        up_pre = (up_active * slope[:, cols]).astype(BF)
        g_in[:, cols] = g_in[:, cols] + jnp.dot(normed_t, up_pre, preferred_element_type=F32)
        part = lax.dot_general(
            up_pre, in_chunk(0, n), (((1,), (1,)), ((), ())), preferred_element_type=F32
        )
        up_normed = part if up_normed is None else up_normed + part
    unit = unit_i[...]
    prod = up_normed * unit
    gsum[0:1, :] = gsum[0:1, :] + jnp.sum(prod, axis=0, keepdims=True)
    up_unit = up_normed * gain[...]
    mean_up = jnp.mean(up_unit, axis=-1, keepdims=True)
    mean_proj = jnp.mean(prod * gain[...], axis=-1, keepdims=True)
    up_conv[...] = inv_i[...] * (up_unit - mean_up - unit * mean_proj)

    @pl.when(step == pl.num_programs(0) - 1)
    def _():
        g_out_t = g_out[...].astype(BF).T
        for x in range(nx):
            for h in range(2):
                hr = jnp.where(me_c == h, 0, 1)
                xr = lax.rem(x - me_x + nx, nx)
                for d in range(dp):
                    lanes = slice(128 * (2 * x + h), 128 * (2 * x + h) + 128)
                    parts[hr, xr, d, :, 0:128] = g_in[d * 16 : d * 16 + 16, lanes].astype(BF)
                    lo = d * per_d + 16 * x
                    parts[hr, xr, d, :, 128:256] = g_out_t[lo : lo + 16, 128 * h : 128 * h + 128]


def pointwise(place, bufs, n_own, n_men, unit, inv, img, gain, s_own, s_men, hid, inv_count):
    pixels, chans = n_own.shape
    nx = len(bufs) // 2
    dp = bufs[0].shape[0]
    tile = 256
    whole = lambda a: pl.BlockSpec(a.shape, lambda t, *_: (0,) * a.ndim)
    rows = lambda w: pl.BlockSpec((tile, w), lambda t, *_: (t, 0))
    return pl.pallas_call(
        functools.partial(pointwise_kernel, nx=nx, inv_count=inv_count),
        out_shape=[
            jax.ShapeDtypeStruct((pixels, chans), BF),
            jax.ShapeDtypeStruct((pixels, chans), F32),
            jax.ShapeDtypeStruct((2, nx, dp, 16, 256), BF),
            jax.ShapeDtypeStruct((8, chans), F32),
        ],
        grid_spec=pltpu.PrefetchScalarGridSpec(
            num_scalar_prefetch=1,
            grid=(pixels // tile,),
            in_specs=[whole(b) for b in bufs]
            + [rows(chans), rows(chans), rows(chans), rows(1), rows(chans)]
            + [whole(gain), whole(s_own), whole(s_men)],
            out_specs=[
                rows(chans),
                rows(chans),
                pl.BlockSpec((2, nx, dp, 16, 256), lambda t, *_: (0, 0, 0, 0, 0)),
                pl.BlockSpec((8, chans), lambda t, *_: (0, 0)),
            ],
            scratch_shapes=[
                pltpu.VMEM((2, hid // 128, chans, 128), BF),
                pltpu.VMEM((2, 2, hid, 128), BF),
                pltpu.VMEM((tile, hid), BF),
                pltpu.VMEM((tile, hid), F32),
                pltpu.VMEM((chans, hid), F32),
                pltpu.VMEM((chans, hid), F32),
            ],
        ),
        name="pointwise",
    )(place, *bufs, n_own, n_men, unit, inv, img, gain, s_own, s_men)


def tap_grad_kernel(img, top, bot, up, gsum, out, pad, *, taps):
    rows, cols, chans = img.shape
    edge = taps // 2
    fill_padded(pad, img, top, bot, edge)
    out[...] = jnp.zeros_like(out)
    for cb in range(chans // 128):
        lanes = slice(cb * 128, cb * 128 + 128)
        for lo, hi in ((0, 4), (4, taps)):

            def block(wb, accs):
                accs = list(accs)
                for u in range(2):
                    w0 = pl.multiple_of(wb * 16 + u * 8, 8)
                    ups = [up[h, pl.ds(w0, 8), lanes] for h in range(rows)]
                    for j in range(lo, hi):
                        for r in range(rows + 2 * edge):
                            v = pad[cb, r, pl.ds(w0 + (LEFT - edge + j), 8), :]
                            for i in range(taps):
                                h = r - i
                                if 0 <= h < rows:
                                    q = (j - lo) * taps + i
                                    accs[q] = accs[q] + v * ups[h]
                return tuple(accs)

            count = (hi - lo) * taps
            accs = lax.fori_loop(
                0, cols // 16, block, tuple(jnp.zeros((8, 128), F32) for _ in range(count))
            )
            for q in range(count):
                tap = (q % taps) * taps + lo + q // taps
                line = jnp.sum(accs[q], axis=0, keepdims=True)
                out[cb, tap : tap + 1, :] = line
        for q in range(2):
            out[cb, taps * taps + q : taps * taps + q + 1, :] = gsum[q : q + 1, lanes]


def tap_grad(img, top, bot, up, gsum, taps):
    rows, cols, chans = img.shape
    edge = taps // 2
    return pl.pallas_call(
        functools.partial(tap_grad_kernel, taps=taps),
        out_shape=jax.ShapeDtypeStruct((chans // 128, 64, 128), F32),
        scratch_shapes=[pltpu.VMEM((chans // 128, rows + 2 * edge, cols + LEFT + 8, 128), F32)],
        name="tap_grad",
    )(img, top, bot, up, gsum)


def total(block):
    return jnp.sum(block.astype(F32), axis=0)


def spread(block, axis):
    copies = jnp.broadcast_to(block[None], (lax.axis_size(axis),) + block.shape)
    return lax.all_to_all(copies, axis, 0, 0, tiled=True)


def body(images, w_in, w_out, kernel, gain, scale):
    pictures = images[0, 0]
    row_count, col_count, channels = pictures.shape
    taps = kernel.shape[1]
    edge = taps // 2
    dp, row = lax.axis_size("dp"), lax.axis_size("row")
    nx = row // 2
    hid = w_in.shape[2]
    inv_count = 1.0 / (images.shape[1] * dp * row_count * row * col_count)
    me = lax.axis_index("row")
    me_x, me_c = me // 2, me % 2
    place = jnp.stack([me_x, me_c]).astype(jnp.int32)

    ends = row - 1
    top = lax.ppermute(pictures[row_count - edge :], "row", [(i, i + 1) for i in range(ends)])
    bot = lax.ppermute(pictures[:edge], "row", [(i + 1, i) for i in range(ends)])

    piece_in = lax.dynamic_slice(w_in[0], (0, 128 * me), (w_in.shape[1], 128))
    piece_out = lax.dynamic_slice(w_out[0], (16 * me_x, 128 * me_c), (16, 128))
    piece = jnp.concatenate([piece_in, piece_out], axis=1)
    small = jnp.concatenate(
        [kernel[0].reshape(taps * taps, channels), gain, scale, jnp.zeros((5, channels), BF)], axis=0
    )
    mentor = lax.ppermute(jnp.concatenate([piece, small], axis=0), "grp", ring("grp", 1))
    line = spread(jnp.concatenate([piece, mentor[:16]], axis=0), "dp")
    hops = [line] + [
        lax.ppermute(line, "row", [(i, (i + 2 * k) % row) for i in range(row)]) for k in range(1, nx)
    ]
    bufs = []
    for block in hops:
        bufs += [block, lax.ppermute(block, "row", [(i, i ^ 1) for i in range(row)])]

    count = taps * taps
    wide = lambda a: a.astype(F32)
    mentor_small = wide(mentor[16:])
    own_gain, own_scale = wide(gain), wide(scale)
    n_own, n_men, unit, inv = conv_norm(
        pictures,
        top,
        bot,
        wide(small[:count]),
        mentor_small[:count],
        own_gain,
        mentor_small[count : count + 1],
        taps,
    )
    feat, up_conv, parts, gsum = pointwise(
        place,
        bufs,
        n_own,
        n_men,
        unit,
        inv,
        pictures.reshape(-1, channels),
        own_gain,
        own_scale,
        mentor_small[count + 1 : count + 2],
        hid,
        inv_count,
    )
    other = lax.ppermute(parts[1], "row", [(i, i ^ 1) for i in range(row)])
    chip = (wide(parts[0]) + wide(other)).astype(BF)
    sent = [
        lax.ppermute(chip[k], "row", [(i, (i + 2 * k) % row) for i in range(row)]) for k in range(1, nx)
    ]
    line_sum = wide(chip[0])
    for block in sent:
        line_sum = line_sum + wide(block)
    line_sum = line_sum.astype(BF)
    taps_out = tap_grad(
        pictures, top, bot, up_conv.reshape(row_count, col_count, channels), gsum, taps
    )
    rest = taps_out.reshape(row, 128 // row, 128).astype(BF)
    rest = total(lax.all_to_all(rest, "row", 0, 0, tiled=True)).astype(BF)
    fill = jnp.concatenate([rest, jnp.zeros_like(rest)], axis=1)
    fill = jnp.broadcast_to(fill[None], (dp,) + fill.shape)
    piece_sum = total(lax.all_to_all(jnp.concatenate([line_sum, fill], axis=1), "dp", 0, 0, tiled=True))
    done = wide(spread(piece_sum.astype(BF), "row"))
    grad_in = done[:, :16, :128].transpose(1, 0, 2).reshape(16, row * 128)
    grad_out = done[:, :16, 128:].reshape(nx, 2, 16, 128).transpose(0, 2, 1, 3).reshape(nx * 16, 256)
    rest = done[:, 16:, :128].reshape(channels // 128, 64, 128)
    rest = rest.transpose(1, 0, 2).reshape(64, channels)
    return (
        feat.reshape(images.shape),
        grad_in[None],
        grad_out[None],
        rest[:count].reshape(1, taps, taps, channels),
        rest[count : count + 1],
        rest[count + 1 : count + 2],
    )


def solution(mesh):
    in_specs = (
        P("grp", "dp", "row", None, None),
        P("grp", "dp", None),
        P("grp", "dp", None),
        P("grp", None, None, None),
        P("grp", None),
        P("grp", None),
    )
    out_specs = in_specs
    return jax.shard_map(body, mesh=mesh, in_specs=in_specs, out_specs=out_specs, check_vma=False)
```

```python
import functools

import jax
import jax.numpy as jnp
from jax import lax
from jax.experimental import pallas as pl
from jax.experimental.pallas import tpu as pltpu
from jax.sharding import PartitionSpec as P

SQRT_HALF = 0.7071067811865476
INV_SQRT_TAU = 0.3989422804014327
BF = jnp.bfloat16
F32 = jnp.float32
LEFT = 8


def ring(axis, shift, size=None):
    count = lax.axis_size(axis)
    return [(i, (i + shift) % count) for i in range(count)]


def fill_padded(pad, img, top, bot, edge):
    rows, cols, chans = img.shape
    zero = jnp.zeros((8, 128), F32)
    for cb in range(chans // 128):
        lanes = slice(cb * 128, cb * 128 + 128)
        for r in range(rows + 2 * edge):
            if r < edge:
                ref, q = top, r
            elif r < rows + edge:
                ref, q = img, r - edge
            else:
                ref, q = bot, r - rows - edge
            pad[cb, r, 0:LEFT, :] = zero
            pad[cb, r, LEFT + cols : LEFT + cols + 8, :] = zero
            pad[cb, r, LEFT : LEFT + cols, :] = ref[q, :, lanes].astype(F32)


def tree(terms):
    while len(terms) > 1:
        terms = [
            terms[a] + terms[a + 1] if a + 1 < len(terms) else terms[a] for a in range(0, len(terms), 2)
        ]
    return terms[0]


def conv_norm_kernel(
    img, top, bot, own, men, n_own, n_men, unit_o, inv_o, pad, filt, wide_taps, *, taps
):
    rows, cols, chans = img.shape
    edge = taps // 2
    fill_padded(pad, img, top, bot, edge)
    for s, small in ((0, own), (1, men)):
        lines = small[...].astype(F32)
        for q in range(taps * taps):
            for cb in range(chans // 128):
                wide_taps[s, cb, q] = jnp.broadcast_to(
                    lines[q : q + 1, cb * 128 : cb * 128 + 128], (16, 128)
                ).astype(BF)
    for cb in range(chans // 128):
        lanes = slice(cb * 128, cb * 128 + 128)

        def block(wb, _):
            w0 = pl.multiple_of(wb * 16, 16)
            accs = {}
            for j in range(taps):
                vs = [
                    pad[cb, r, pl.ds(w0 + (LEFT - edge + j), 16), :].astype(BF)
                    for r in range(rows + 2 * edge)
                ]
                for s in range(2):
                    w = [wide_taps[s, cb, i * taps + j] for i in range(taps)]
                    for h in range(rows):
                        term = tree([vs[h + i] * w[i] for i in range(taps)]).astype(F32)
                        accs[s, h] = term if j == 0 else accs[s, h] + term
            for h in range(rows):
                for s in range(2):
                    filt[s, h, pl.ds(w0, 16), lanes] = accs[s, h]
            return 0

        lax.fori_loop(0, cols // 16, block, 0)
    span = 256
    for s, small, normed in ((0, own, n_own), (1, men, n_men)):
        gain = small[taps * taps : taps * taps + 1, :].astype(F32)

        def norm(t, _):
            h = t // (cols // span)
            w0 = pl.multiple_of((t % (cols // span)) * span, span)
            at = pl.multiple_of(t * span, span)
            x = filt[s, h, pl.ds(w0, span), :]
            centred = x - jnp.mean(x, axis=-1, keepdims=True)
            inv = lax.rsqrt(jnp.mean(centred * centred, axis=-1, keepdims=True) + 1e-06)
            unit = centred * inv
            normed[pl.ds(at, span), :] = (unit * gain).astype(BF)
            if s == 0:
                unit_o[pl.ds(at, span), :] = unit
                inv_o[pl.ds(at, span), :] = inv
            return 0

        lax.fori_loop(0, rows * cols // span, norm, 0)


def conv_norm(img, top, bot, own, men, taps):
    rows, cols, chans = img.shape
    edge = taps // 2
    pixels = rows * cols
    return pl.pallas_call(
        functools.partial(conv_norm_kernel, taps=taps),
        out_shape=[
            jax.ShapeDtypeStruct((pixels, chans), BF),
            jax.ShapeDtypeStruct((pixels, chans), BF),
            jax.ShapeDtypeStruct((pixels, chans), F32),
            jax.ShapeDtypeStruct((pixels, 1), F32),
        ],
        scratch_shapes=[
            pltpu.VMEM((chans // 128, rows + 2 * edge, cols + LEFT + 8, 128), F32),
            pltpu.VMEM((2, rows, cols, chans), F32),
            pltpu.VMEM((2, chans // 128, taps * taps, 16, 128), BF),
        ],
        name="conv_norm",
    )(img, top, bot, own, men)


def pointwise_kernel(place, *refs, nx, count, inv_count):
    bufs = refs[: 2 * nx]
    (n_own, n_men, unit_i, inv_i, img, own, men) = refs[2 * nx : 2 * nx + 7]
    (feat, up_conv, keep, send, gsum) = refs[2 * nx + 7 : 2 * nx + 12]
    (w_in, w_out, act, slope, g_in, g_out) = refs[2 * nx + 12 :]
    gain = own[count : count + 1, :].astype(F32)
    s_own = own[count + 1 : count + 2, :].astype(F32)
    s_men = men[count + 1 : count + 2, :].astype(F32)
    step = pl.program_id(0)
    tile, chans = n_own.shape
    hid = w_out.shape[2]
    dp = bufs[0].shape[0]
    chunks = hid // 256
    me_x, me_c = place[0], place[1]
    per_d = hid // dp

    @pl.when(step == 0)
    def _():
        for k in range(nx):
            x = lax.rem(me_x - k + nx, nx)
            for c in range(2):
                h = me_c if c == 0 else 1 - me_c
                buf = bufs[2 * k + c]
                for d in range(dp):
                    for s in range(2):
                        w_in[s, 2 * x + h, d * 16 : d * 16 + 16, :] = buf[d, s * 16 : s * 16 + 16, 0:128]
                        w_out[s, h, pl.ds(pl.multiple_of(d * per_d + x * 16, 16), 16), :] = buf[
                            d, s * 16 : s * 16 + 16, 128:256
                        ]
        g_in[...] = jnp.zeros_like(g_in)
        g_out[...] = jnp.zeros_like(g_out)
        gsum[...] = jnp.zeros_like(gsum)

    def in_chunk(s, n):
        return jnp.concatenate([w_in[s, 2 * n], w_in[s, 2 * n + 1]], axis=1)

    def out_chunk(s, n):
        rows = slice(n * 256, n * 256 + 256)
        return jnp.concatenate([w_out[s, 0, rows, :], w_out[s, 1, rows, :]], axis=1)

    branch = [None, None]
    for s, normed in ((0, n_own), (1, n_men)):
        x = normed[...]
        for n in range(chunks):
            pre = jnp.dot(x, in_chunk(s, n), preferred_element_type=F32)
            half_cdf = 0.5 + 0.5 * lax.erf(pre * SQRT_HALF)
            activated = (pre * half_cdf).astype(BF)
            if s == 0:
                act[:, n * 256 : n * 256 + 256] = activated
                slope[:, n * 256 : n * 256 + 256] = (
                    half_cdf + pre * jnp.exp(-0.5 * pre * pre) * INV_SQRT_TAU
                )
            part = jnp.dot(activated, out_chunk(s, n), preferred_element_type=F32)
            branch[s] = part if branch[s] is None else branch[s] + part
    scaled = branch[0] * s_own
    feat[...] = (img[...].astype(F32) + scaled).astype(BF)
    upstream = (scaled - s_men[...] * branch[1]) * inv_count
    gsum[1:2, :] = gsum[1:2, :] + jnp.sum(upstream * branch[0], axis=0, keepdims=True)
    up_branch = (upstream * s_own).astype(BF)
    up_branch_t = up_branch.T
    normed_t = n_own[...].T
    up_normed = None
    for n in range(chunks):
        cols = slice(n * 256, n * 256 + 256)
        g_out[:, cols] = g_out[:, cols] + jnp.dot(up_branch_t, act[:, cols], preferred_element_type=F32)
        up_active = lax.dot_general(
            up_branch, out_chunk(0, n), (((1,), (1,)), ((), ())), preferred_element_type=F32
        )
        up_pre = (up_active * slope[:, cols]).astype(BF)
        g_in[:, cols] = g_in[:, cols] + jnp.dot(normed_t, up_pre, preferred_element_type=F32)
        part = lax.dot_general(
            up_pre, in_chunk(0, n), (((1,), (1,)), ((), ())), preferred_element_type=F32
        )
        up_normed = part if up_normed is None else up_normed + part
    unit = unit_i[...]
    prod = up_normed * unit
    gsum[0:1, :] = gsum[0:1, :] + jnp.sum(prod, axis=0, keepdims=True)
    up_unit = up_normed * gain
    mean_up = jnp.mean(up_unit, axis=-1, keepdims=True)
    mean_proj = jnp.mean(prod * gain, axis=-1, keepdims=True)
    up_conv[...] = inv_i[...] * (up_unit - mean_up - unit * mean_proj)

    @pl.when(step == pl.num_programs(0) - 1)
    def _():
        g_out_t = g_out[...].astype(BF).T
        for x in range(nx):
            for h in range(2):
                xr = lax.rem(x - me_x + nx, nx)
                lanes = slice(128 * (2 * x + h), 128 * (2 * x + h) + 128)

                def emit(out):
                    for d in range(dp):
                        out[xr, d, :, 0:128] = g_in[d * 16 : d * 16 + 16, lanes].astype(BF)
                        lo = d * per_d + 16 * x
                        out[xr, d, :, 128:256] = g_out_t[lo : lo + 16, 128 * h : 128 * h + 128]

                pl.when(me_c == h)(functools.partial(emit, keep))
                pl.when(me_c != h)(functools.partial(emit, send))


def pointwise(place, bufs, n_own, n_men, unit, inv, img, own, men, hid, count, inv_count):
    pixels, chans = n_own.shape
    nx = len(bufs) // 2
    dp = bufs[0].shape[0]
    tile = 512
    whole = lambda a: pl.BlockSpec(a.shape, lambda t, *_: (0,) * a.ndim)
    rows = lambda w: pl.BlockSpec((tile, w), lambda t, *_: (t, 0))
    return pl.pallas_call(
        functools.partial(pointwise_kernel, nx=nx, count=count, inv_count=inv_count),
        out_shape=[
            jax.ShapeDtypeStruct((pixels, chans), BF),
            jax.ShapeDtypeStruct((pixels, chans), F32),
            jax.ShapeDtypeStruct((nx, dp, 16, 256), BF),
            jax.ShapeDtypeStruct((nx, dp, 16, 256), BF),
            jax.ShapeDtypeStruct((8, chans), F32),
        ],
        grid_spec=pltpu.PrefetchScalarGridSpec(
            num_scalar_prefetch=1,
            grid=(pixels // tile,),
            in_specs=[whole(b) for b in bufs]
            + [rows(chans), rows(chans), rows(chans), rows(1), rows(chans)]
            + [whole(own), whole(men)],
            out_specs=[
                rows(chans),
                rows(chans),
                pl.BlockSpec((nx, dp, 16, 256), lambda t, *_: (0, 0, 0, 0)),
                pl.BlockSpec((nx, dp, 16, 256), lambda t, *_: (0, 0, 0, 0)),
                pl.BlockSpec((8, chans), lambda t, *_: (0, 0)),
            ],
            scratch_shapes=[
                pltpu.VMEM((2, hid // 128, chans, 128), BF),
                pltpu.VMEM((2, 2, hid, 128), BF),
                pltpu.VMEM((tile, hid), BF),
                pltpu.VMEM((tile, hid), F32),
                pltpu.VMEM((chans, hid), F32),
                pltpu.VMEM((chans, hid), F32),
            ],
        ),
        name="pointwise",
    )(place, *bufs, n_own, n_men, unit, inv, img, own, men)


def tap_grad_kernel(img, top, bot, up, gsum, out, pad, lines, *, taps):
    rows, cols, chans = img.shape
    edge = taps // 2
    fill_padded(pad, img, top, bot, edge)
    lines[...] = jnp.zeros_like(lines)
    for cb in range(chans // 128):
        lanes = slice(cb * 128, cb * 128 + 128)
        for lo, hi in ((0, 4), (4, taps)):

            def block(wb, accs):
                accs = list(accs)
                for u in range(2):
                    w0 = pl.multiple_of(wb * 32 + u * 16, 16)
                    ups = [up[h, pl.ds(w0, 16), lanes].astype(BF) for h in range(rows)]
                    for j in range(lo, hi):
                        vs = [
                            pad[cb, r, pl.ds(w0 + (LEFT - edge + j), 16), :].astype(BF)
                            for r in range(rows + 2 * edge)
                        ]
                        for i in range(taps):
                            term = tree([vs[h + i] * ups[h] for h in range(rows)]).astype(F32)
                            q = (j - lo) * taps + i
                            accs[q] = accs[q] + (term[:8] + term[8:])
                return tuple(accs)

            count = (hi - lo) * taps
            accs = lax.fori_loop(
                0, cols // 32, block, tuple(jnp.zeros((8, 128), F32) for _ in range(count))
            )
            for q in range(count):
                tap = (q % taps) * taps + lo + q // taps
                lines[cb, tap : tap + 1, :] = jnp.sum(accs[q], axis=0, keepdims=True)
        for q in range(2):
            lines[cb, taps * taps + q : taps * taps + q + 1, :] = gsum[q : q + 1, lanes]
    out[...] = lines[...].astype(BF)


def tap_grad(img, top, bot, up, gsum, taps):
    rows, cols, chans = img.shape
    edge = taps // 2
    return pl.pallas_call(
        functools.partial(tap_grad_kernel, taps=taps),
        out_shape=jax.ShapeDtypeStruct((chans // 128, 64, 128), BF),
        scratch_shapes=[
            pltpu.VMEM((chans // 128, rows + 2 * edge, cols + LEFT + 8, 128), F32),
            pltpu.VMEM((chans // 128, 64, 128), F32),
        ],
        name="tap_grad",
    )(img, top, bot, up, gsum)


def total(block):
    return jnp.sum(block.astype(F32), axis=0)


def spread(block, axis):
    copies = jnp.broadcast_to(block[None], (lax.axis_size(axis),) + block.shape)
    return lax.all_to_all(copies, axis, 0, 0, tiled=True)


def body(images, w_in, w_out, kernel, gain, scale):
    pictures = images[0, 0]
    row_count, col_count, channels = pictures.shape
    taps = kernel.shape[1]
    edge = taps // 2
    dp, row = lax.axis_size("dp"), lax.axis_size("row")
    nx = row // 2
    hid = w_in.shape[2]
    inv_count = 1.0 / (images.shape[1] * dp * row_count * row * col_count)
    me = lax.axis_index("row")
    me_x, me_c = me // 2, me % 2
    place = jnp.stack([me_x, me_c]).astype(jnp.int32)

    ends = row - 1
    top = lax.ppermute(pictures[row_count - edge :], "row", [(i, i + 1) for i in range(ends)])
    bot = lax.ppermute(pictures[:edge], "row", [(i + 1, i) for i in range(ends)])

    piece_in = lax.dynamic_slice(w_in[0], (0, 128 * me), (w_in.shape[1], 128))
    piece_out = lax.dynamic_slice(w_out[0], (16 * me_x, 128 * me_c), (16, 128))
    piece = jnp.concatenate([piece_in, piece_out], axis=1)
    small = jnp.concatenate(
        [kernel[0].reshape(taps * taps, channels), gain, scale, jnp.zeros((5, channels), BF)], axis=0
    )
    mentor = lax.ppermute(jnp.concatenate([piece, small], axis=0), "grp", ring("grp", 1))
    line = spread(jnp.concatenate([piece, mentor[:16]], axis=0), "dp")
    hops = [line] + [
        lax.ppermute(line, "row", [(i, (i + 2 * k) % row) for i in range(row)]) for k in range(1, nx)
    ]
    bufs = []
    for block in hops:
        bufs += [block, lax.ppermute(block, "row", [(i, i ^ 1) for i in range(row)])]

    count = taps * taps
    wide = lambda a: a.astype(F32)
    men_small = mentor[16:]
    n_own, n_men, unit, inv = conv_norm(pictures, top, bot, small, men_small, taps)
    feat, up_conv, keep, send, gsum = pointwise(
        place,
        bufs,
        n_own,
        n_men,
        unit,
        inv,
        pictures.reshape(-1, channels),
        small,
        men_small,
        hid,
        count,
        inv_count,
    )
    other = lax.ppermute(send, "row", [(i, i ^ 1) for i in range(row)])
    chip = (wide(keep) + wide(other)).astype(BF)
    sent = [
        lax.ppermute(chip[k], "row", [(i, (i + 2 * k) % row) for i in range(row)]) for k in range(1, nx)
    ]
    line_sum = wide(chip[0])
    for block in sent:
        line_sum = line_sum + wide(block)
    line_sum = line_sum.astype(BF)
    taps_out = tap_grad(
        pictures, top, bot, up_conv.reshape(row_count, col_count, channels), gsum, taps
    )
    rest = taps_out.reshape(row, 128 // row, 128)
    rest = total(lax.all_to_all(rest, "row", 0, 0, tiled=True)).astype(BF)
    fill = jnp.concatenate([rest, jnp.zeros_like(rest)], axis=1)
    fill = jnp.broadcast_to(fill[None], (dp,) + fill.shape)
    piece_sum = total(lax.all_to_all(jnp.concatenate([line_sum, fill], axis=1), "dp", 0, 0, tiled=True))
    done = wide(spread(piece_sum.astype(BF), "row"))
    grad_in = done[:, :16, :128].transpose(1, 0, 2).reshape(16, row * 128)
    grad_out = done[:, :16, 128:].reshape(nx, 2, 16, 128).transpose(0, 2, 1, 3).reshape(nx * 16, 256)
    rest = done[:, 16:, :128].reshape(channels // 128, 64, 128)
    rest = rest.transpose(1, 0, 2).reshape(64, channels)
    return (
        feat.reshape(images.shape),
        grad_in[None],
        grad_out[None],
        rest[:count].reshape(1, taps, taps, channels),
        rest[count : count + 1],
        rest[count + 1 : count + 2],
    )


def solution(mesh):
    in_specs = (
        P("grp", "dp", "row", None, None),
        P("grp", "dp", None),
        P("grp", "dp", None),
        P("grp", None, None, None),
        P("grp", None),
        P("grp", None),
    )
    out_specs = in_specs
    return jax.shard_map(body, mesh=mesh, in_specs=in_specs, out_specs=out_specs, check_vma=False)
```

```python
import functools

import jax
import jax.numpy as jnp
from jax import lax
from jax.experimental import pallas as pl
from jax.experimental.pallas import tpu as pltpu
from jax.sharding import PartitionSpec as P


SQRT_HALF = 0.7071067811865476
INV_SQRT_TAU = 0.3989422804014327
BF = jnp.bfloat16
F32 = jnp.float32
LEFT = 8


def ring(axis, shift):
    count = lax.axis_size(axis)
    return [(i, (i + shift) % count) for i in range(count)]


def prep_kernel(images, w_in, w_out, kernel, gain, scale, head, tail, piece, small, lines, sems, *, edge):
    rows = images.shape[2]
    up = pltpu.make_async_copy(images.at[0, 0, pl.ds(0, edge)], head, sems.at[0])
    down = pltpu.make_async_copy(images.at[0, 0, pl.ds(rows - edge, edge)], tail, sems.at[1])
    up.start()
    down.start()
    me = lax.axis_index("row")
    me_x, me_c = lax.div(me, 2), lax.rem(me, 2)
    part_in = w_in[0, :, pl.ds(pl.multiple_of(128 * me, 128), 128)]
    part_out = w_out[0, pl.ds(pl.multiple_of(16 * me_x, 16), 16), pl.ds(pl.multiple_of(128 * me_c, 128), 128)]
    for q in range(piece.shape[0]):
        piece[q, :, 0:128] = part_in
        piece[q, :, 128:256] = part_out
    taps = kernel.shape[1]
    lines[...] = jnp.zeros_like(lines)
    for i in range(taps):
        lines[i * taps : i * taps + taps, :] = kernel[0, i].astype(F32)
    lines[taps * taps : taps * taps + 1, :] = gain[...].astype(F32)
    lines[taps * taps + 1 : taps * taps + 2, :] = scale[...].astype(F32)
    small[...] = lines[...].astype(BF)
    up.wait()
    down.wait()


def prep(images, w_in, w_out, kernel, gain, scale, copies):
    cols, chans = images.shape[3:]
    edge = kernel.shape[1] // 2
    anywhere = pl.BlockSpec(memory_space=pl.ANY)
    vmem = pl.BlockSpec(memory_space=pltpu.VMEM)
    return pl.pallas_call(
        functools.partial(prep_kernel, edge=edge),
        out_shape=[
            jax.ShapeDtypeStruct((edge, cols, chans), BF),
            jax.ShapeDtypeStruct((edge, cols, chans), BF),
            jax.ShapeDtypeStruct((copies, 16, 256), BF),
            jax.ShapeDtypeStruct((64, chans), BF),
        ],
        in_specs=[anywhere] + [vmem] * 5,
        out_specs=[anywhere, anywhere, vmem, vmem],
        scratch_shapes=[pltpu.VMEM((64, chans), F32), pltpu.SemaphoreType.DMA((2,))],
        name="prep",
    )(images, w_in, w_out, kernel, gain, scale)


def finish_kernel(done, grad_in, grad_out, grad_kern, grad_gain, grad_scale, lines):
    row = done.shape[0]
    taps = grad_kern.shape[1]
    for r in range(row):
        grad_in[0, :, 128 * r : 128 * r + 128] = done[r, 0:16, 0:128].astype(F32)
        x, h = r // 2, r % 2
        grad_out[0, 16 * x : 16 * x + 16, 128 * h : 128 * h + 128] = done[r, 0:16, 128:256].astype(F32)
        lines[8 * r : 8 * r + 8, :] = done[r, 16:24, :].astype(F32)
    for i in range(taps):
        grad_kern[0, i] = lines[i * taps : i * taps + taps, :]
    grad_gain[...] = lines[taps * taps : taps * taps + 1, :]
    grad_scale[...] = lines[taps * taps + 1 : taps * taps + 2, :]


def finish(done, taps):
    row, _, chans = done.shape
    return pl.pallas_call(
        finish_kernel,
        out_shape=[
            jax.ShapeDtypeStruct((1, 16, 128 * row), F32),
            jax.ShapeDtypeStruct((1, 8 * row, 256), F32),
            jax.ShapeDtypeStruct((1, taps, taps, chans), F32),
            jax.ShapeDtypeStruct((1, chans), F32),
            jax.ShapeDtypeStruct((1, chans), F32),
        ],
        scratch_shapes=[pltpu.VMEM((8 * row, chans), F32)],
        name="finish",
    )(done)


def fill_padded(pad, img, top, bot, edge):
    rows, cols, chans = img.shape
    zero = jnp.zeros((8, 128), F32)
    for cb in range(chans // 128):
        lanes = slice(cb * 128, cb * 128 + 128)
        for r in range(rows + 2 * edge):
            if r < edge:
                ref, q = top, r
            elif r < rows + edge:
                ref, q = img, r - edge
            else:
                ref, q = bot, r - rows - edge
            pad[cb, r, 0:LEFT, :] = zero
            pad[cb, r, LEFT + cols : LEFT + cols + 8, :] = zero
            pad[cb, r, LEFT : LEFT + cols, :] = ref[q, :, lanes].astype(F32)


def tree(terms):
    while len(terms) > 1:
        terms = [
            terms[a] + terms[a + 1] if a + 1 < len(terms) else terms[a] for a in range(0, len(terms), 2)
        ]
    return terms[0]


def conv_kernel(img, top, bot, own, men, filt, pad, wide_taps, *, taps):
    rows, _, _ = img.shape
    edge = taps // 2
    span = filt.shape[2]
    base = pl.program_id(0) * span

    @pl.when(pl.program_id(0) == 0)
    def _():
        fill_padded(pad, img, top, bot, edge)
        for s, small in ((0, own), (1, men)):
            lines = small[...].astype(F32)
            for q in range(taps * taps):
                wide_taps[s, q] = jnp.broadcast_to(lines[q : q + 1, :], (16, 128)).astype(BF)

    def block(wb, _):
        at = pl.multiple_of(wb * 16, 16)
        w0 = pl.multiple_of(base + at, 16)
        accs = {}
        for j in range(taps):
            vs = [
                pad[0, r, pl.ds(w0 + (LEFT - edge + j), 16), :].astype(BF) for r in range(rows + 2 * edge)
            ]
            for s in range(2):
                w = [wide_taps[s, i * taps + j] for i in range(taps)]
                for h in range(rows):
                    term = tree([vs[h + i] * w[i] for i in range(taps)]).astype(F32)
                    accs[s, h] = term if j == 0 else accs[s, h] + term
        for h in range(rows):
            for s in range(2):
                filt[s, h, pl.ds(at, 16), :] = accs[s, h]
        return 0

    lax.fori_loop(0, span // 16, block, 0)


def conv(img, top, bot, own, men, taps, cb):
    rows, cols, _ = img.shape
    edge = taps // 2
    lanes = lambda a: pl.BlockSpec(a.shape[:-1] + (128,), lambda t: (0,) * (a.ndim - 1) + (cb,))
    return pl.pallas_call(
        functools.partial(conv_kernel, taps=taps),
        out_shape=jax.ShapeDtypeStruct((2, rows, cols, 128), F32),
        grid=(4,),
        in_specs=[lanes(img), lanes(top), lanes(bot), lanes(own), lanes(men)],
        out_specs=pl.BlockSpec((2, rows, cols // 4, 128), lambda t: (0, 0, t, 0)),
        scratch_shapes=[
            pltpu.VMEM((1, rows + 2 * edge, cols + LEFT + 8, 128), F32),
            pltpu.VMEM((2, taps * taps, 16, 128), BF),
        ],
    )(img, top, bot, own, men)


def pointwise_kernel(*refs, nx, count, inv_count):
    bufs = refs[: 2 * nx]
    (filt_a, filt_b, img, own, men) = refs[2 * nx : 2 * nx + 5]
    (feat, up_conv, keep, send, gsum) = refs[2 * nx + 5 : 2 * nx + 10]
    (w_in, w_out, act, slope, g_in, g_out) = refs[2 * nx + 10 :]
    gain = own[count : count + 1, :].astype(F32)
    s_own = own[count + 1 : count + 2, :].astype(F32)
    s_men = men[count + 1 : count + 2, :].astype(F32)
    step = pl.program_id(0)
    tile, _ = img.shape
    hid = w_out.shape[2]
    dp = bufs[0].shape[0] // 2
    chunks = hid // 256
    me, me_g = lax.axis_index("row"), lax.axis_index("grp")
    me_x, me_c = lax.div(me, 2), lax.rem(me, 2)
    per_d = hid // dp

    @pl.when(step == 0)
    def _():
        for k in range(nx):
            x = lax.rem(me_x - k + nx, nx)
            for c in range(2):
                h = me_c if c == 0 else 1 - me_c
                buf = bufs[2 * k + c]
                for d in range(dp):
                    for s in range(2):
                        q = dp * (me_g if s == 0 else 1 - me_g) + d
                        w_in[s, 2 * x + h, d * 16 : d * 16 + 16, :] = buf[q, :, 0:128]
                        at = pl.multiple_of(d * per_d + x * 16, 16)
                        w_out[s, h, pl.ds(at, 16), :] = buf[q, :, 128:256]
        g_in[...] = jnp.zeros_like(g_in)
        g_out[...] = jnp.zeros_like(g_out)
        gsum[...] = jnp.zeros_like(gsum)

    def in_chunk(s, n):
        return jnp.concatenate([w_in[s, 2 * n], w_in[s, 2 * n + 1]], axis=1)

    def out_chunk(s, n):
        rows = slice(n * 256, n * 256 + 256)
        return jnp.concatenate([w_out[s, 0, rows, :], w_out[s, 1, rows, :]], axis=1)

    branch = [None, None]
    for s, small in ((0, own), (1, men)):
        x = jnp.concatenate([filt_a[s].reshape(tile, 128), filt_b[s].reshape(tile, 128)], axis=1)
        centred = x - jnp.mean(x, axis=-1, keepdims=True)
        inv = lax.rsqrt(jnp.mean(centred * centred, axis=-1, keepdims=True) + 1e-06)
        x = centred * inv
        if s == 0:
            unit, inv_std = x, inv
        x = (x * small[count : count + 1, :].astype(F32)).astype(BF)
        if s == 0:
            normed_t = x.T
        for n in range(chunks):
            pre = jnp.dot(x, in_chunk(s, n), preferred_element_type=F32)
            half_cdf = 0.5 + 0.5 * lax.erf(pre * SQRT_HALF)
            activated = (pre * half_cdf).astype(BF)
            if s == 0:
                act[:, n * 256 : n * 256 + 256] = activated
                slope[:, n * 256 : n * 256 + 256] = (
                    half_cdf + pre * jnp.exp(-0.5 * pre * pre) * INV_SQRT_TAU
                )
            part = jnp.dot(activated, out_chunk(s, n), preferred_element_type=F32)
            branch[s] = part if branch[s] is None else branch[s] + part
    scaled = branch[0] * s_own
    feat[...] = (img[...].astype(F32) + scaled).astype(BF)
    upstream = (scaled - s_men[...] * branch[1]) * inv_count
    gsum[1:2, :] = gsum[1:2, :] + jnp.sum(upstream * branch[0], axis=0, keepdims=True)
    up_branch = (upstream * s_own).astype(BF)
    up_branch_t = up_branch.T
    up_normed = None
    for n in range(chunks):
        cols = slice(n * 256, n * 256 + 256)
        g_out[:, cols] = g_out[:, cols] + jnp.dot(up_branch_t, act[:, cols], preferred_element_type=F32)
        up_active = lax.dot_general(
            up_branch, out_chunk(0, n), (((1,), (1,)), ((), ())), preferred_element_type=F32
        )
        up_pre = (up_active * slope[:, cols]).astype(BF)
        g_in[:, cols] = g_in[:, cols] + jnp.dot(normed_t, up_pre, preferred_element_type=F32)
        part = lax.dot_general(
            up_pre, in_chunk(0, n), (((1,), (1,)), ((), ())), preferred_element_type=F32
        )
        up_normed = part if up_normed is None else up_normed + part
    prod = up_normed * unit
    gsum[0:1, :] = gsum[0:1, :] + jnp.sum(prod, axis=0, keepdims=True)
    up_unit = up_normed * gain
    mean_up = jnp.mean(up_unit, axis=-1, keepdims=True)
    mean_proj = jnp.mean(prod * gain, axis=-1, keepdims=True)
    up_conv[...] = inv_std * (up_unit - mean_up - unit * mean_proj)

    @pl.when(step == pl.num_programs(0) - 1)
    def _():
        g_out_t = g_out[...].astype(BF).T
        for x in range(nx):
            for h in range(2):
                xr = lax.rem(x - me_x + nx, nx)
                lanes = slice(128 * (2 * x + h), 128 * (2 * x + h) + 128)

                def emit(out):
                    for d in range(dp):
                        out[xr, d, :, 0:128] = g_in[d * 16 : d * 16 + 16, lanes].astype(BF)
                        lo = d * per_d + 16 * x
                        out[xr, d, :, 128:256] = g_out_t[lo : lo + 16, 128 * h : 128 * h + 128]

                pl.when(me_c == h)(functools.partial(emit, keep))
                pl.when(me_c != h)(functools.partial(emit, send))


def pointwise(bufs, filt_a, filt_b, img, own, men, hid, count, inv_count):
    pixels, chans = img.shape
    _, _, cols, _ = filt_a.shape
    nx = len(bufs) // 2
    dp = bufs[0].shape[0] // 2
    tile = 512
    whole = lambda a: pl.BlockSpec(a.shape, lambda t: (0,) * a.ndim)
    lines = pl.BlockSpec((tile, chans), lambda t: (t, 0))
    filt = pl.BlockSpec((2, tile // cols, cols, 128), lambda t: (0, t, 0, 0))
    part = pl.BlockSpec((nx, dp, 16, 256), lambda t: (0, 0, 0, 0))
    return pl.pallas_call(
        functools.partial(pointwise_kernel, nx=nx, count=count, inv_count=inv_count),
        out_shape=[
            jax.ShapeDtypeStruct((pixels, chans), BF),
            jax.ShapeDtypeStruct((pixels, chans), F32),
            jax.ShapeDtypeStruct((nx, dp, 16, 256), BF),
            jax.ShapeDtypeStruct((nx, dp, 16, 256), BF),
            jax.ShapeDtypeStruct((8, chans), F32),
        ],
        grid=(pixels // tile,),
        in_specs=[whole(b) for b in bufs] + [filt, filt, lines, whole(own), whole(men)],
        out_specs=[lines, lines, part, part, pl.BlockSpec((8, chans), lambda t: (0, 0))],
        scratch_shapes=[
            pltpu.VMEM((2, hid // 128, chans, 128), BF),
            pltpu.VMEM((2, 2, hid, 128), BF),
            pltpu.VMEM((tile, hid), BF),
            pltpu.VMEM((tile, hid), F32),
            pltpu.VMEM((chans, hid), F32),
            pltpu.VMEM((chans, hid), F32),
        ],
        name="pointwise",
    )(*bufs, filt_a, filt_b, img, own, men)


def tap_grad_kernel(img, top, bot, up, gsum, out, pad, lines, *, taps):
    rows, cols, chans = img.shape
    edge = taps // 2
    fill_padded(pad, img, top, bot, edge)
    lines[...] = jnp.zeros_like(lines)
    for cb in range(chans // 128):
        lanes = slice(cb * 128, cb * 128 + 128)
        for lo, hi in ((0, 4), (4, taps)):

            def block(wb, accs):
                accs = list(accs)
                for u in range(2):
                    w0 = pl.multiple_of(wb * 32 + u * 16, 16)
                    ups = [up[h, pl.ds(w0, 16), lanes].astype(BF) for h in range(rows)]
                    for j in range(lo, hi):
                        vs = [
                            pad[cb, r, pl.ds(w0 + (LEFT - edge + j), 16), :].astype(BF)
                            for r in range(rows + 2 * edge)
                        ]
                        for i in range(taps):
                            term = tree([vs[h + i] * ups[h] for h in range(rows)]).astype(F32)
                            q = (j - lo) * taps + i
                            accs[q] = accs[q] + (term[:8] + term[8:])
                return tuple(accs)

            count = (hi - lo) * taps
            accs = lax.fori_loop(
                0, cols // 32, block, tuple(jnp.zeros((8, 128), F32) for _ in range(count))
            )
            for q in range(count):
                tap = (q % taps) * taps + lo + q // taps
                lines[tap : tap + 1, lanes] = jnp.sum(accs[q], axis=0, keepdims=True)
        for q in range(2):
            lines[taps * taps + q : taps * taps + q + 1, lanes] = gsum[q : q + 1, lanes]
    out[...] = lines[...].astype(BF)


def tap_grad(img, top, bot, up, gsum, taps):
    rows, cols, chans = img.shape
    edge = taps // 2
    return pl.pallas_call(
        functools.partial(tap_grad_kernel, taps=taps),
        out_shape=jax.ShapeDtypeStruct((64, chans), BF),
        scratch_shapes=[
            pltpu.VMEM((chans // 128, rows + 2 * edge, cols + LEFT + 8, 128), F32),
            pltpu.VMEM((64, chans), F32),
        ],
        name="tap_grad",
    )(img, top, bot, up, gsum)


def total(block):
    return jnp.sum(block.astype(F32), axis=0)


def spread(block, axis):
    copies = jnp.broadcast_to(block[None], (lax.axis_size(axis),) + block.shape)
    return lax.all_to_all(copies, axis, 0, 0, tiled=True)


def step(images, w_in, w_out, kernel, gain, scale):
    pictures = images[0, 0]
    row_count, col_count, channels = pictures.shape
    taps = kernel.shape[1]
    count = taps * taps
    dp, row, grp = lax.axis_size("dp"), lax.axis_size("row"), lax.axis_size("grp")
    nx = row // 2
    hid = w_in.shape[2]
    inv_count = 1.0 / (images.shape[1] * dp * row_count * row * col_count)
    twin = [(i, i ^ 1) for i in range(row)]
    chips = lambda k: [(i, (i + 2 * k) % row) for i in range(row)]

    head, tail, piece, small = prep(images, w_in, w_out, kernel, gain, scale, grp * dp)
    top = lax.ppermute(tail, "row", [(i, i + 1) for i in range(row - 1)])
    bot = lax.ppermute(head, "row", [(i + 1, i) for i in range(row - 1)])
    men_small = lax.ppermute(small, "grp", ring("grp", 1))
    line = lax.all_to_all(piece, ("grp", "dp"), 0, 0, tiled=True)
    hops = [line] + [lax.ppermute(line, "row", chips(k)) for k in range(1, nx)]
    bufs = []
    for block in hops:
        bufs += [block, lax.ppermute(block, "row", twin)]

    filt_a = conv(pictures, top, bot, small, men_small, taps, 0)
    filt_b = conv(pictures, top, bot, small, men_small, taps, 1)
    feat, up_conv, keep, send, gsum = pointwise(
        bufs, filt_a, filt_b, pictures.reshape(-1, channels), small, men_small, hid, count, inv_count
    )
    wide = lambda a: a.astype(F32)
    other = lax.ppermute(send, "row", twin)
    chip = (wide(keep) + wide(other)).astype(BF)
    sent = [lax.ppermute(chip[k], "row", chips(k)) for k in range(1, nx)]
    line_sum = wide(chip[0])
    for block in sent:
        line_sum = line_sum + wide(block)
    line_sum = line_sum.astype(BF)
    rest = tap_grad(pictures, top, bot, up_conv.reshape(row_count, col_count, channels), gsum, taps)
    rest = rest.reshape(row, 64 // row, channels)
    rest = total(lax.all_to_all(rest, "row", 0, 0, tiled=True)).astype(BF)
    rest = jnp.broadcast_to(rest[None], (dp,) + rest.shape)
    piece_sum = total(lax.all_to_all(jnp.concatenate([line_sum, rest], axis=1), "dp", 0, 0, tiled=True))
    grads = finish(spread(piece_sum.astype(BF), "row"), taps)
    return (feat.reshape(images.shape), *grads)


def solution(mesh):
    in_specs = (
        P("grp", "dp", "row", None, None),
        P("grp", "dp", None),
        P("grp", "dp", None),
        P("grp", None, None, None),
        P("grp", None),
        P("grp", None),
    )
    out_specs = in_specs
    return jax.shard_map(step, mesh=mesh, in_specs=in_specs, out_specs=out_specs, check_vma=False)
```

```python
import functools

import jax
import jax.numpy as jnp
from jax import lax
from jax.experimental import pallas as pl
from jax.experimental.pallas import tpu as pltpu
from jax.sharding import PartitionSpec as P


SQRT_HALF = 0.7071067811865476
INV_SQRT_TAU = 0.3989422804014327
BF = jnp.bfloat16
F32 = jnp.float32
LEFT = 8


def ring(axis, shift):
    count = lax.axis_size(axis)
    return [(i, (i + shift) % count) for i in range(count)]


def prep_kernel(images, w_in, w_out, kernel, gain, scale, head, tail, piece, small, lines, sems, *, edge):
    rows = images.shape[2]
    up = pltpu.make_async_copy(images.at[0, 0, pl.ds(0, edge)], head, sems.at[0])
    down = pltpu.make_async_copy(images.at[0, 0, pl.ds(rows - edge, edge)], tail, sems.at[1])
    up.start()
    down.start()
    me = lax.axis_index("row")
    me_x, me_c = lax.div(me, 2), lax.rem(me, 2)
    part_in = w_in[0, :, pl.ds(pl.multiple_of(128 * me, 128), 128)]
    part_out = w_out[0, pl.ds(pl.multiple_of(16 * me_x, 16), 16), pl.ds(pl.multiple_of(128 * me_c, 128), 128)]
    for q in range(piece.shape[0]):
        piece[q, :, 0:128] = part_in
        piece[q, :, 128:256] = part_out
    taps = kernel.shape[1]
    lines[...] = jnp.zeros_like(lines)
    for i in range(taps):
        lines[i * taps : i * taps + taps, :] = kernel[0, i].astype(F32)
    lines[taps * taps : taps * taps + 1, :] = gain[...].astype(F32)
    lines[taps * taps + 1 : taps * taps + 2, :] = scale[...].astype(F32)
    small[...] = lines[...].astype(BF)
    up.wait()
    down.wait()


def prep(images, w_in, w_out, kernel, gain, scale, copies):
    cols, chans = images.shape[3:]
    edge = kernel.shape[1] // 2
    anywhere = pl.BlockSpec(memory_space=pl.ANY)
    vmem = pl.BlockSpec(memory_space=pltpu.VMEM)
    return pl.pallas_call(
        functools.partial(prep_kernel, edge=edge),
        out_shape=[
            jax.ShapeDtypeStruct((edge, cols, chans), BF),
            jax.ShapeDtypeStruct((edge, cols, chans), BF),
            jax.ShapeDtypeStruct((copies, 16, 256), BF),
            jax.ShapeDtypeStruct((64, chans), BF),
        ],
        in_specs=[anywhere] + [vmem] * 5,
        out_specs=[vmem] * 4,
        scratch_shapes=[pltpu.VMEM((64, chans), F32), pltpu.SemaphoreType.DMA((2,))],
        name="prep",
    )(images, w_in, w_out, kernel, gain, scale)


def finish_kernel(done, grad_in, grad_out, grad_kern, grad_gain, grad_scale, lines):
    row = done.shape[0]
    taps = grad_kern.shape[0]
    for r in range(row):
        grad_in[0, :, 128 * r : 128 * r + 128] = done[r, 0:16, 0:128].astype(F32)
        x, h = r // 2, r % 2
        grad_out[0, 16 * x : 16 * x + 16, 128 * h : 128 * h + 128] = done[r, 0:16, 128:256].astype(F32)
        lines[8 * r : 8 * r + 8, :] = done[r, 16:24, :].astype(F32)
    for q in range(taps * taps):
        grad_kern[q // taps, q % taps] = lines[q : q + 1, :]
    grad_gain[...] = lines[taps * taps : taps * taps + 1, :]
    grad_scale[...] = lines[taps * taps + 1 : taps * taps + 2, :]


def finish(done, taps):
    row, _, chans = done.shape
    return pl.pallas_call(
        finish_kernel,
        out_shape=[
            jax.ShapeDtypeStruct((1, 16, 128 * row), F32),
            jax.ShapeDtypeStruct((1, 8 * row, 256), F32),
            jax.ShapeDtypeStruct((taps, taps, 1, chans), F32),
            jax.ShapeDtypeStruct((1, chans), F32),
            jax.ShapeDtypeStruct((1, chans), F32),
        ],
        scratch_shapes=[pltpu.VMEM((8 * row, chans), F32)],
        name="finish",
    )(done)


def fill_padded(pad, img, top, bot, edge):
    rows, cols, chans = img.shape
    zero = jnp.zeros((8, 128), F32)
    for cb in range(chans // 128):
        lanes = slice(cb * 128, cb * 128 + 128)
        for r in range(rows + 2 * edge):
            if r < edge:
                ref, q = top, r
            elif r < rows + edge:
                ref, q = img, r - edge
            else:
                ref, q = bot, r - rows - edge
            pad[cb, r, 0:LEFT, :] = zero
            pad[cb, r, LEFT + cols : LEFT + cols + 8, :] = zero
            pad[cb, r, LEFT : LEFT + cols, :] = ref[q, :, lanes].astype(F32)


def tree(terms):
    while len(terms) > 1:
        terms = [
            terms[a] + terms[a + 1] if a + 1 < len(terms) else terms[a] for a in range(0, len(terms), 2)
        ]
    return terms[0]


def conv_kernel(img, top, bot, own, men, filt, pad, wide_taps, *, taps):
    rows, _, _ = img.shape
    edge = taps // 2
    span = filt.shape[2]
    base = pl.program_id(0) * span

    @pl.when(pl.program_id(0) == 0)
    def _():
        fill_padded(pad, img, top, bot, edge)
        for s, small in ((0, own), (1, men)):
            lines = small[...].astype(F32)
            for q in range(taps * taps):
                wide_taps[s, q] = jnp.broadcast_to(lines[q : q + 1, :], (16, 128)).astype(BF)

    def block(wb, _):
        at = pl.multiple_of(wb * 16, 16)
        w0 = pl.multiple_of(base + at, 16)
        accs = {}
        for j in range(taps):
            vs = [
                pad[0, r, pl.ds(w0 + (LEFT - edge + j), 16), :].astype(BF) for r in range(rows + 2 * edge)
            ]
            for s in range(2):
                w = [wide_taps[s, i * taps + j] for i in range(taps)]
                for h in range(rows):
                    term = tree([vs[h + i] * w[i] for i in range(taps)]).astype(F32)
                    accs[s, h] = term if j == 0 else accs[s, h] + term
        for h in range(rows):
            for s in range(2):
                filt[s, h, pl.ds(at, 16), :] = accs[s, h]
        return 0

    lax.fori_loop(0, span // 16, block, 0)


def conv(img, top, bot, own, men, taps, cb):
    rows, cols, _ = img.shape
    edge = taps // 2
    lanes = lambda a: pl.BlockSpec(a.shape[:-1] + (128,), lambda t: (0,) * (a.ndim - 1) + (cb,))
    return pl.pallas_call(
        functools.partial(conv_kernel, taps=taps),
        out_shape=jax.ShapeDtypeStruct((2, rows, cols, 128), F32),
        grid=(4,),
        in_specs=[lanes(img), lanes(top), lanes(bot), lanes(own), lanes(men)],
        out_specs=pl.BlockSpec((2, rows, cols // 4, 128), lambda t: (0, 0, t, 0)),
        scratch_shapes=[
            pltpu.VMEM((1, rows + 2 * edge, cols + LEFT + 8, 128), F32),
            pltpu.VMEM((2, taps * taps, 16, 128), BF),
        ],
    )(img, top, bot, own, men)


def pointwise_kernel(*refs, nx, count, inv_count):
    bufs = refs[: 2 * nx]
    (filt_a, filt_b, img, own, men) = refs[2 * nx : 2 * nx + 5]
    (feat, up_conv, keep, send, gsum) = refs[2 * nx + 5 : 2 * nx + 10]
    (w_in, w_out, act, slope, g_in, g_out) = refs[2 * nx + 10 :]
    gain = own[count : count + 1, :].astype(F32)
    s_own = own[count + 1 : count + 2, :].astype(F32)
    s_men = men[count + 1 : count + 2, :].astype(F32)
    step = pl.program_id(0)
    tile, _ = img.shape
    hid = w_out.shape[2]
    dp = bufs[0].shape[0] // 2
    chunks = hid // 256
    me, me_g = lax.axis_index("row"), lax.axis_index("grp")
    me_x, me_c = lax.div(me, 2), lax.rem(me, 2)
    per_d = hid // dp

    @pl.when(step == 0)
    def _():
        for k in range(nx):
            x = lax.rem(me_x - k + nx, nx)
            for c in range(2):
                h = me_c if c == 0 else 1 - me_c
                buf = bufs[2 * k + c]
                for d in range(dp):
                    for s in range(2):
                        q = dp * (me_g if s == 0 else 1 - me_g) + d
                        w_in[s, 2 * x + h, d * 16 : d * 16 + 16, :] = buf[q, :, 0:128]
                        at = pl.multiple_of(d * per_d + x * 16, 16)
                        w_out[s, h, pl.ds(at, 16), :] = buf[q, :, 128:256]
        g_in[...] = jnp.zeros_like(g_in)
        g_out[...] = jnp.zeros_like(g_out)
        gsum[...] = jnp.zeros_like(gsum)

    def in_chunk(s, n):
        return jnp.concatenate([w_in[s, 2 * n], w_in[s, 2 * n + 1]], axis=1)

    def out_chunk(s, n):
        rows = slice(n * 256, n * 256 + 256)
        return jnp.concatenate([w_out[s, 0, rows, :], w_out[s, 1, rows, :]], axis=1)

    branch = [None, None]
    for s, small in ((0, own), (1, men)):
        x = jnp.concatenate([filt_a[s].reshape(tile, 128), filt_b[s].reshape(tile, 128)], axis=1)
        centred = x - jnp.mean(x, axis=-1, keepdims=True)
        inv = lax.rsqrt(jnp.mean(centred * centred, axis=-1, keepdims=True) + 1e-06)
        x = centred * inv
        if s == 0:
            unit, inv_std = x, inv
        x = (x * small[count : count + 1, :].astype(F32)).astype(BF)
        if s == 0:
            normed_t = x.T
        for n in range(chunks):
            pre = jnp.dot(x, in_chunk(s, n), preferred_element_type=F32)
            half_cdf = 0.5 + 0.5 * lax.erf(pre * SQRT_HALF)
            activated = (pre * half_cdf).astype(BF)
            if s == 0:
                act[:, n * 256 : n * 256 + 256] = activated
                slope[:, n * 256 : n * 256 + 256] = (
                    half_cdf + pre * jnp.exp(-0.5 * pre * pre) * INV_SQRT_TAU
                )
            part = jnp.dot(activated, out_chunk(s, n), preferred_element_type=F32)
            branch[s] = part if branch[s] is None else branch[s] + part
    scaled = branch[0] * s_own
    feat[...] = (img[...].astype(F32) + scaled).astype(BF)
    upstream = (scaled - s_men[...] * branch[1]) * inv_count
    gsum[1:2, :] = gsum[1:2, :] + jnp.sum(upstream * branch[0], axis=0, keepdims=True)
    up_branch = (upstream * s_own).astype(BF)
    up_branch_t = up_branch.T
    up_normed = None
    for n in range(chunks):
        cols = slice(n * 256, n * 256 + 256)
        g_out[:, cols] = g_out[:, cols] + jnp.dot(up_branch_t, act[:, cols], preferred_element_type=F32)
        up_active = lax.dot_general(
            up_branch, out_chunk(0, n), (((1,), (1,)), ((), ())), preferred_element_type=F32
        )
        up_pre = (up_active * slope[:, cols]).astype(BF)
        g_in[:, cols] = g_in[:, cols] + jnp.dot(normed_t, up_pre, preferred_element_type=F32)
        part = lax.dot_general(
            up_pre, in_chunk(0, n), (((1,), (1,)), ((), ())), preferred_element_type=F32
        )
        up_normed = part if up_normed is None else up_normed + part
    prod = up_normed * unit
    gsum[0:1, :] = gsum[0:1, :] + jnp.sum(prod, axis=0, keepdims=True)
    up_unit = up_normed * gain
    mean_up = jnp.mean(up_unit, axis=-1, keepdims=True)
    mean_proj = jnp.mean(prod * gain, axis=-1, keepdims=True)
    up_conv[...] = inv_std * (up_unit - mean_up - unit * mean_proj)

    @pl.when(step == pl.num_programs(0) - 1)
    def _():
        g_out_t = g_out[...].astype(BF).T
        for x in range(nx):
            for h in range(2):
                xr = lax.rem(x - me_x + nx, nx)
                lanes = slice(128 * (2 * x + h), 128 * (2 * x + h) + 128)

                def emit(out):
                    for d in range(dp):
                        out[xr, d, :, 0:128] = g_in[d * 16 : d * 16 + 16, lanes].astype(BF)
                        lo = d * per_d + 16 * x
                        out[xr, d, :, 128:256] = g_out_t[lo : lo + 16, 128 * h : 128 * h + 128]

                pl.when(me_c == h)(functools.partial(emit, keep))
                pl.when(me_c != h)(functools.partial(emit, send))


def pointwise(bufs, filt_a, filt_b, img, own, men, hid, count, inv_count):
    pixels, chans = img.shape
    _, _, cols, _ = filt_a.shape
    nx = len(bufs) // 2
    dp = bufs[0].shape[0] // 2
    tile = 512
    whole = lambda a: pl.BlockSpec(a.shape, lambda t: (0,) * a.ndim)
    lines = pl.BlockSpec((tile, chans), lambda t: (t, 0))
    filt = pl.BlockSpec((2, tile // cols, cols, 128), lambda t: (0, t, 0, 0))
    part = pl.BlockSpec((nx, dp, 16, 256), lambda t: (0, 0, 0, 0))
    return pl.pallas_call(
        functools.partial(pointwise_kernel, nx=nx, count=count, inv_count=inv_count),
        out_shape=[
            jax.ShapeDtypeStruct((pixels, chans), BF),
            jax.ShapeDtypeStruct((pixels, chans), F32),
            jax.ShapeDtypeStruct((nx, dp, 16, 256), BF),
            jax.ShapeDtypeStruct((nx, dp, 16, 256), BF),
            jax.ShapeDtypeStruct((8, chans), F32),
        ],
        grid=(pixels // tile,),
        in_specs=[whole(b) for b in bufs] + [filt, filt, lines, whole(own), whole(men)],
        out_specs=[lines, lines, part, part, pl.BlockSpec((8, chans), lambda t: (0, 0))],
        scratch_shapes=[
            pltpu.VMEM((2, hid // 128, chans, 128), BF),
            pltpu.VMEM((2, 2, hid, 128), BF),
            pltpu.VMEM((tile, hid), BF),
            pltpu.VMEM((tile, hid), F32),
            pltpu.VMEM((chans, hid), F32),
            pltpu.VMEM((chans, hid), F32),
        ],
        name="pointwise",
    )(*bufs, filt_a, filt_b, img, own, men)


def tap_grad_kernel(img, top, bot, up, gsum, out, pad, lines, *, taps):
    rows, cols, chans = img.shape
    edge = taps // 2
    fill_padded(pad, img, top, bot, edge)
    lines[...] = jnp.zeros_like(lines)
    for cb in range(chans // 128):
        lanes = slice(cb * 128, cb * 128 + 128)
        for lo, hi in ((0, 4), (4, taps)):

            def block(wb, accs):
                accs = list(accs)
                for u in range(2):
                    w0 = pl.multiple_of(wb * 32 + u * 16, 16)
                    ups = [up[h, pl.ds(w0, 16), lanes].astype(BF) for h in range(rows)]
                    for j in range(lo, hi):
                        vs = [
                            pad[cb, r, pl.ds(w0 + (LEFT - edge + j), 16), :].astype(BF)
                            for r in range(rows + 2 * edge)
                        ]
                        for i in range(taps):
                            term = tree([vs[h + i] * ups[h] for h in range(rows)]).astype(F32)
                            q = (j - lo) * taps + i
                            accs[q] = accs[q] + (term[:8] + term[8:])
                return tuple(accs)

            count = (hi - lo) * taps
            accs = lax.fori_loop(
                0, cols // 32, block, tuple(jnp.zeros((8, 128), F32) for _ in range(count))
            )
            for q in range(count):
                tap = (q % taps) * taps + lo + q // taps
                lines[tap : tap + 1, lanes] = jnp.sum(accs[q], axis=0, keepdims=True)
        for q in range(2):
            lines[taps * taps + q : taps * taps + q + 1, lanes] = gsum[q : q + 1, lanes]
    out[...] = lines[...].astype(BF)


def tap_grad(img, top, bot, up, gsum, taps):
    rows, cols, chans = img.shape
    edge = taps // 2
    return pl.pallas_call(
        functools.partial(tap_grad_kernel, taps=taps),
        out_shape=jax.ShapeDtypeStruct((64, chans), BF),
        scratch_shapes=[
            pltpu.VMEM((chans // 128, rows + 2 * edge, cols + LEFT + 8, 128), F32),
            pltpu.VMEM((64, chans), F32),
        ],
        name="tap_grad",
    )(img, top, bot, up, gsum)


def total(block):
    return jnp.sum(block.astype(F32), axis=0)


def spread(block, axis):
    copies = jnp.broadcast_to(block[None], (lax.axis_size(axis),) + block.shape)
    return lax.all_to_all(copies, axis, 0, 0, tiled=True)


def step(images, w_in, w_out, kernel, gain, scale):
    pictures = images[0, 0]
    row_count, col_count, channels = pictures.shape
    taps = kernel.shape[1]
    count = taps * taps
    dp, row, grp = lax.axis_size("dp"), lax.axis_size("row"), lax.axis_size("grp")
    nx = row // 2
    hid = w_in.shape[2]
    inv_count = 1.0 / (images.shape[1] * dp * row_count * row * col_count)
    twin = [(i, i ^ 1) for i in range(row)]
    chips = lambda k: [(i, (i + 2 * k) % row) for i in range(row)]

    head, tail, piece, small = prep(images, w_in, w_out, kernel, gain, scale, grp * dp)
    top = lax.ppermute(tail, "row", [(i, i + 1) for i in range(row - 1)])
    bot = lax.ppermute(head, "row", [(i + 1, i) for i in range(row - 1)])
    men_small = lax.ppermute(small, "grp", ring("grp", 1))
    line = lax.all_to_all(piece, ("grp", "dp"), 0, 0, tiled=True)
    hops = [line] + [lax.ppermute(line, "row", chips(k)) for k in range(1, nx)]
    bufs = []
    for block in hops:
        bufs += [block, lax.ppermute(block, "row", twin)]

    filt_a = conv(pictures, top, bot, small, men_small, taps, 0)
    filt_b = conv(pictures, top, bot, small, men_small, taps, 1)
    feat, up_conv, keep, send, gsum = pointwise(
        bufs, filt_a, filt_b, pictures.reshape(-1, channels), small, men_small, hid, count, inv_count
    )
    wide = lambda a: a.astype(F32)
    other = lax.ppermute(send, "row", twin)
    chip = (wide(keep) + wide(other)).astype(BF)
    sent = [lax.ppermute(chip[k], "row", chips(k)) for k in range(1, nx)]
    line_sum = wide(chip[0])
    for block in sent:
        line_sum = line_sum + wide(block)
    line_sum = line_sum.astype(BF)
    rest = tap_grad(pictures, top, bot, up_conv.reshape(row_count, col_count, channels), gsum, taps)
    rest = rest.reshape(row, 64 // row, channels)
    rest = total(lax.all_to_all(rest, "row", 0, 0, tiled=True)).astype(BF)
    rest = jnp.broadcast_to(rest[None], (dp,) + rest.shape)
    piece_sum = total(lax.all_to_all(jnp.concatenate([line_sum, rest], axis=1), "dp", 0, 0, tiled=True))
    grad_in, grad_out, grad_kern, *rest = finish(spread(piece_sum.astype(BF), "row"), taps)
    return (feat.reshape(images.shape), grad_in, grad_out, grad_kern.transpose(2, 0, 1, 3), *rest)


def solution(mesh):
    in_specs = (
        P("grp", "dp", "row", None, None),
        P("grp", "dp", None),
        P("grp", "dp", None),
        P("grp", None, None, None),
        P("grp", None),
        P("grp", None),
    )
    out_specs = in_specs
    return jax.shard_map(step, mesh=mesh, in_specs=in_specs, out_specs=out_specs, check_vma=False)
```

```python
import functools

import jax
import jax.numpy as jnp
from jax import lax
from jax.experimental import pallas as pl
from jax.experimental.pallas import tpu as pltpu
from jax.sharding import PartitionSpec as P


SQRT_HALF = 0.7071067811865476
INV_SQRT_TAU = 0.3989422804014327
BF = jnp.bfloat16
F32 = jnp.float32
SUB = 512
TILE = 512
LEFT = 8


def ring(axis, shift):
    count = lax.axis_size(axis)
    return [(i, (i + shift) % count) for i in range(count)]


def prep_kernel(images, w_in, w_out, kernel, gain, scale, head, tail, piece, small, lines, sems, *, edge):
    rows = images.shape[2]
    up = pltpu.make_async_copy(images.at[0, 0, pl.ds(0, edge)], head, sems.at[0])
    down = pltpu.make_async_copy(images.at[0, 0, pl.ds(rows - edge, edge)], tail, sems.at[1])
    up.start()
    down.start()
    me = lax.axis_index("row")
    me_x, me_c = lax.div(me, 2), lax.rem(me, 2)
    part_in = w_in[0, :, pl.ds(pl.multiple_of(128 * me, 128), 128)]
    part_out = w_out[0, pl.ds(pl.multiple_of(16 * me_x, 16), 16), pl.ds(pl.multiple_of(128 * me_c, 128), 128)]
    for q in range(piece.shape[0]):
        piece[q, :, 0:128] = part_in
        piece[q, :, 128:256] = part_out
    taps = kernel.shape[1]
    lines[...] = jnp.zeros_like(lines)
    for i in range(taps):
        lines[i * taps : i * taps + taps, :] = kernel[0, i].astype(F32)
    lines[taps * taps : taps * taps + 1, :] = gain[...].astype(F32)
    lines[taps * taps + 1 : taps * taps + 2, :] = scale[...].astype(F32)
    small[...] = lines[...].astype(BF)
    up.wait()
    down.wait()


def prep(images, w_in, w_out, kernel, gain, scale, copies):
    cols, chans = images.shape[3:]
    edge = kernel.shape[1] // 2
    anywhere = pl.BlockSpec(memory_space=pl.ANY)
    vmem = pl.BlockSpec(memory_space=pltpu.VMEM)
    return pl.pallas_call(
        functools.partial(prep_kernel, edge=edge),
        out_shape=[
            jax.ShapeDtypeStruct((edge, cols, chans), BF),
            jax.ShapeDtypeStruct((edge, cols, chans), BF),
            jax.ShapeDtypeStruct((copies, 16, 256), BF),
            jax.ShapeDtypeStruct((64, chans), BF),
        ],
        in_specs=[anywhere] + [vmem] * 5,
        out_specs=[vmem] * 4,
        scratch_shapes=[pltpu.VMEM((64, chans), F32), pltpu.SemaphoreType.DMA((2,))],
        name="prep",
    )(images, w_in, w_out, kernel, gain, scale)


def finish_kernel(done, grad_in, grad_out, grad_kern, grad_gain, grad_scale, lines):
    row = done.shape[0]
    taps = grad_kern.shape[0]
    for r in range(row):
        grad_in[0, :, 128 * r : 128 * r + 128] = done[r, 0:16, 0:128].astype(F32)
        x, h = r // 2, r % 2
        grad_out[0, 16 * x : 16 * x + 16, 128 * h : 128 * h + 128] = done[r, 0:16, 128:256].astype(F32)
        lines[8 * r : 8 * r + 8, :] = done[r, 16:24, :].astype(F32)
    for q in range(taps * taps):
        grad_kern[q // taps, q % taps] = lines[q : q + 1, :]
    grad_gain[...] = lines[taps * taps : taps * taps + 1, :]
    grad_scale[...] = lines[taps * taps + 1 : taps * taps + 2, :]


def finish(done, taps):
    row, _, chans = done.shape
    return pl.pallas_call(
        finish_kernel,
        out_shape=[
            jax.ShapeDtypeStruct((1, 16, 128 * row), F32),
            jax.ShapeDtypeStruct((1, 8 * row, 256), F32),
            jax.ShapeDtypeStruct((taps, taps, 1, chans), F32),
            jax.ShapeDtypeStruct((1, chans), F32),
            jax.ShapeDtypeStruct((1, chans), F32),
        ],
        scratch_shapes=[pltpu.VMEM((8 * row, chans), F32)],
        name="finish",
    )(done)


def fill_padded(pad, img, top, bot, edge):
    rows, cols, chans = img.shape
    zero = jnp.zeros((8, 128), F32)
    for cb in range(chans // 128):
        lanes = slice(cb * 128, cb * 128 + 128)
        for r in range(rows + 2 * edge):
            if r < edge:
                ref, q = top, r
            elif r < rows + edge:
                ref, q = img, r - edge
            else:
                ref, q = bot, r - rows - edge
            pad[cb, r, 0:LEFT, :] = zero
            pad[cb, r, LEFT + cols : LEFT + cols + 8, :] = zero
            pad[cb, r, LEFT : LEFT + cols, :] = ref[q, :, lanes].astype(F32)


def tree(terms):
    while len(terms) > 1:
        terms = [
            terms[a] + terms[a + 1] if a + 1 < len(terms) else terms[a] for a in range(0, len(terms), 2)
        ]
    return terms[0]


def conv_kernel(img, top, bot, own, men, filt, pad, wide_taps, *, taps):
    rows, _, _ = img.shape
    edge = taps // 2
    span = filt.shape[2]
    base = pl.program_id(0) * span

    @pl.when(pl.program_id(0) == 0)
    def _():
        fill_padded(pad, img, top, bot, edge)
        for s, small in ((0, own), (1, men)):
            lines = small[...].astype(F32)
            for q in range(taps * taps):
                wide_taps[s, q] = jnp.broadcast_to(lines[q : q + 1, :], (16, 128)).astype(BF)

    def block(wb, _):
        at = pl.multiple_of(wb * 16, 16)
        w0 = pl.multiple_of(base + at, 16)
        accs = {}
        for j in range(taps):
            vs = [
                pad[0, r, pl.ds(w0 + (LEFT - edge + j), 16), :].astype(BF) for r in range(rows + 2 * edge)
            ]
            for s in range(2):
                w = [wide_taps[s, i * taps + j] for i in range(taps)]
                for h in range(rows):
                    term = tree([vs[h + i] * w[i] for i in range(taps)]).astype(F32)
                    accs[s, h] = term if j == 0 else accs[s, h] + term
        for h in range(rows):
            for s in range(2):
                filt[s, h, pl.ds(at, 16), :] = accs[s, h]
        return 0

    lax.fori_loop(0, span // 16, block, 0)


def conv(img, top, bot, own, men, taps, cb):
    rows, cols, _ = img.shape
    edge = taps // 2
    lanes = lambda a: pl.BlockSpec(a.shape[:-1] + (128,), lambda t: (0,) * (a.ndim - 1) + (cb,))
    return pl.pallas_call(
        functools.partial(conv_kernel, taps=taps),
        out_shape=jax.ShapeDtypeStruct((2, rows, cols, 128), F32),
        grid=(4,),
        in_specs=[lanes(img), lanes(top), lanes(bot), lanes(own), lanes(men)],
        out_specs=pl.BlockSpec((2, rows, cols // 4, 128), lambda t: (0, 0, t, 0)),
        scratch_shapes=[
            pltpu.VMEM((1, rows + 2 * edge, cols + LEFT + 8, 128), F32),
            pltpu.VMEM((2, taps * taps, 16, 128), BF),
        ],
    )(img, top, bot, own, men)


def tap_grad(img, top, bot, up, gsum, pad, lines, taps):
    rows, cols, chans = img.shape
    edge = taps // 2
    fill_padded(pad, img, top, bot, edge)
    lines[...] = jnp.zeros_like(lines)
    for cb in range(chans // 128):
        lanes = slice(cb * 128, cb * 128 + 128)
        for lo, hi in ((0, 4), (4, taps)):

            def block(wb, accs):
                accs = list(accs)
                for u in range(2):
                    w0 = pl.multiple_of(wb * 32 + u * 16, 16)
                    ups = [up[h, pl.ds(w0, 16), lanes] for h in range(rows)]
                    for j in range(lo, hi):
                        vs = [
                            pad[cb, r, pl.ds(w0 + (LEFT - edge + j), 16), :].astype(BF)
                            for r in range(rows + 2 * edge)
                        ]
                        for i in range(taps):
                            term = tree([vs[h + i] * ups[h] for h in range(rows)]).astype(F32)
                            q = (j - lo) * taps + i
                            accs[q] = accs[q] + (term[:8] + term[8:])
                return tuple(accs)

            count = (hi - lo) * taps
            accs = lax.fori_loop(
                0, cols // 32, block, tuple(jnp.zeros((8, 128), F32) for _ in range(count))
            )
            for q in range(count):
                tap = (q % taps) * taps + lo + q // taps
                lines[tap : tap + 1, lanes] = jnp.sum(accs[q], axis=0, keepdims=True)
        for q in range(2):
            lines[taps * taps + q : taps * taps + q + 1, lanes] = gsum[q : q + 1, lanes]


def pointwise_kernel(*refs, nx, taps, inv_count):
    count = taps * taps
    bufs = refs[: 2 * nx]
    (filt_a, filt_b, img, top, bot, own, men) = refs[2 * nx : 2 * nx + 7]
    (feat, keep, send) = refs[2 * nx + 7 : 2 * nx + 10]
    (w_in, w_out, act, slope, g_in, g_out, normed, up_branch, up_pre, unit_s, up_conv, gsum, pad, lines) = refs[2 * nx + 10 :]
    gain = own[count : count + 1, :].astype(F32)
    s_own = own[count + 1 : count + 2, :].astype(F32)
    s_men = men[count + 1 : count + 2, :].astype(F32)
    step = pl.program_id(0)
    _, cols, chans = img.shape
    tile = feat.shape[0]
    hid = w_out.shape[2]
    dp = bufs[0].shape[0] // 2
    chunks = hid // 256
    me, me_g = lax.axis_index("row"), lax.axis_index("grp")
    me_x, me_c = lax.div(me, 2), lax.rem(me, 2)
    per_d = hid // dp

    @pl.when(step == 0)
    def _():
        for k in range(nx):
            x = lax.rem(me_x - k + nx, nx)
            for c in range(2):
                h = me_c if c == 0 else 1 - me_c
                buf = bufs[2 * k + c]
                for d in range(dp):
                    for s in range(2):
                        q = dp * (me_g if s == 0 else 1 - me_g) + d
                        w_in[s, 2 * x + h, d * 16 : d * 16 + 16, :] = buf[q, :, 0:128]
                        at = pl.multiple_of(d * per_d + x * 16, 16)
                        w_out[s, h, pl.ds(at, 16), :] = buf[q, :, 128:256]
        g_in[...] = jnp.zeros_like(g_in)
        g_out[...] = jnp.zeros_like(g_out)
        gsum[...] = jnp.zeros_like(gsum)

    def in_chunk(s, n):
        return jnp.concatenate([w_in[s, 2 * n], w_in[s, 2 * n + 1]], axis=1)

    def out_chunk(s, n):
        rows = slice(n * 256, n * 256 + 256)
        return jnp.concatenate([w_out[s, 0, rows, :], w_out[s, 1, rows, :]], axis=1)

    per_row = max(1, cols // SUB)

    def block(m, _):
        at = pl.multiple_of(m * SUB, SUB)
        line, w0 = (lax.div(m, per_row), pl.multiple_of(lax.rem(m, per_row) * SUB, SUB)) if SUB <= cols else (pl.ds(m * (SUB // cols), SUB // cols), 0)
        here = pl.ds(at, SUB)
        branch = [None, None]
        for s, small in ((0, own), (1, men)):
            x = jnp.concatenate([f[s, line, pl.ds(w0, min(SUB, cols)), :].reshape(SUB, 128) for f in (filt_a, filt_b)], axis=1)
            centred = x - jnp.mean(x, axis=-1, keepdims=True)
            inv = lax.rsqrt(jnp.mean(centred * centred, axis=-1, keepdims=True) + 1e-06)
            x = centred * inv
            if s == 0:
                unit_s[...] = x
                inv_std = inv
            x = (x * small[count : count + 1, :].astype(F32)).astype(BF)
            if s == 0:
                normed[here, :] = x
            for n in range(chunks):
                pre = jnp.dot(x, in_chunk(s, n), preferred_element_type=F32)
                half_cdf = 0.5 + 0.5 * lax.erf(pre * SQRT_HALF)
                activated = (pre * half_cdf).astype(BF)
                if s == 0:
                    act[here, n * 256 : n * 256 + 256] = activated
                    slope[:, n * 256 : n * 256 + 256] = (
                        half_cdf + pre * jnp.exp(-0.5 * pre * pre) * INV_SQRT_TAU
                    )
                part = jnp.dot(activated, out_chunk(s, n), preferred_element_type=F32)
                branch[s] = part if branch[s] is None else branch[s] + part
        scaled = branch[0] * s_own
        feat[here, :] = (img[pl.ds(step * (tile // cols), tile // cols)].reshape(tile, chans).astype(F32) + scaled).astype(BF)
        upstream = (scaled - s_men * branch[1]) * inv_count
        gsum[1:2, :] = gsum[1:2, :] + jnp.sum(upstream * branch[0], axis=0, keepdims=True)
        back = (upstream * s_own).astype(BF)
        up_branch[here, :] = back
        up_normed = None
        for n in range(chunks):
            lanes = slice(n * 256, n * 256 + 256)
            up_active = lax.dot_general(
                back, out_chunk(0, n), (((1,), (1,)), ((), ())), preferred_element_type=F32
            )
            up_p = (up_active * slope[:, lanes]).astype(BF)
            up_pre[here, lanes] = up_p
            part = lax.dot_general(
                up_p, in_chunk(0, n), (((1,), (1,)), ((), ())), preferred_element_type=F32
            )
            up_normed = part if up_normed is None else up_normed + part
        unit = unit_s[...]
        prod = up_normed * unit
        gsum[0:1, :] = gsum[0:1, :] + jnp.sum(prod, axis=0, keepdims=True)
        up_unit = up_normed * gain
        mean_up = jnp.mean(up_unit, axis=-1, keepdims=True)
        mean_proj = jnp.mean(prod * gain, axis=-1, keepdims=True)
        slab = (inv_std * (up_unit - mean_up - unit * mean_proj)).astype(BF)
        up_conv[pl.ds(step * (tile // cols), tile // cols)] = slab.reshape(tile // cols, cols, chans)
        return 0

    lax.fori_loop(0, tile // SUB, block, 0)
    normed_t = normed[...].T
    up_branch_t = up_branch[...].T
    for n in range(chunks):
        lanes = slice(n * 256, n * 256 + 256)
        g_out[:, lanes] = g_out[:, lanes] + jnp.dot(up_branch_t, act[:, lanes], preferred_element_type=F32)
        g_in[:, lanes] = g_in[:, lanes] + jnp.dot(normed_t, up_pre[:, lanes], preferred_element_type=F32)

    @pl.when(step == pl.num_programs(0) - 1)
    def _():
        tap_grad(img, top, bot, up_conv, gsum, pad, lines, taps)
        g_out_t = g_out[...].astype(BF).T
        for x in range(nx):
            for h in range(2):
                xr = lax.rem(x - me_x + nx, nx)
                lanes = slice(128 * (2 * x + h), 128 * (2 * x + h) + 128)

                def emit(out):
                    for d in range(dp):
                        to = slice(d * 16, d * 16 + 16)
                        out[xr, to, 0:128] = g_in[to, lanes].astype(BF)
                        lo = d * per_d + 16 * x
                        out[xr, to, 128:256] = g_out_t[lo : lo + 16, 128 * h : 128 * h + 128]
                    r = 2 * x + h
                    out[xr, dp * 16 : dp * 16 + 8, :] = lines[8 * r : 8 * r + 8, :].astype(BF)

                pl.when(me_c == h)(functools.partial(emit, keep))
                pl.when(me_c != h)(functools.partial(emit, send))


def pointwise(bufs, filt_a, filt_b, img, top, bot, own, men, hid, taps, inv_count):
    rows, cols, chans = img.shape
    pixels = rows * cols
    nx = len(bufs) // 2
    dp = bufs[0].shape[0] // 2
    edge = taps // 2
    tile = TILE
    whole = lambda a: pl.BlockSpec(a.shape, lambda t: (0,) * a.ndim)
    filt = pl.BlockSpec((2, tile // cols, cols, 128), lambda t: (0, t, 0, 0))
    part = pl.BlockSpec((nx, dp * 16 + 8, 256), lambda t: (0, 0, 0))
    return pl.pallas_call(
        functools.partial(pointwise_kernel, nx=nx, taps=taps, inv_count=inv_count),
        out_shape=[
            jax.ShapeDtypeStruct((pixels, chans), BF),
            jax.ShapeDtypeStruct((nx, dp * 16 + 8, 256), BF),
            jax.ShapeDtypeStruct((nx, dp * 16 + 8, 256), BF),
        ],
        grid=(pixels // tile,),
        in_specs=[whole(b) for b in bufs] + [filt, filt] + [whole(a) for a in (img, top, bot, own, men)],
        out_specs=[pl.BlockSpec((tile, chans), lambda t: (t, 0)), part, part],
        scratch_shapes=[
            pltpu.VMEM((2, hid // 128, chans, 128), BF),
            pltpu.VMEM((2, 2, hid, 128), BF),
            pltpu.VMEM((tile, hid), BF),
            pltpu.VMEM((SUB, hid), F32),
            pltpu.VMEM((chans, hid), F32),
            pltpu.VMEM((chans, hid), F32),
            pltpu.VMEM((tile, chans), BF),
            pltpu.VMEM((tile, chans), BF),
            pltpu.VMEM((tile, hid), BF),
            pltpu.VMEM((SUB, chans), F32),
            pltpu.VMEM((rows, cols, chans), BF),
            pltpu.VMEM((8, chans), F32),
            pltpu.VMEM((chans // 128, rows + 2 * edge, cols + LEFT + 8, 128), F32),
            pltpu.VMEM((64, chans), F32),
        ],
        name="pointwise",
    )(*bufs, filt_a, filt_b, img, top, bot, own, men)


def total(block):
    return jnp.sum(block.astype(F32), axis=0)


def spread(block, axis):
    copies = jnp.broadcast_to(block[None], (lax.axis_size(axis),) + block.shape)
    return lax.all_to_all(copies, axis, 0, 0, tiled=True)


def step(images, w_in, w_out, kernel, gain, scale):
    pictures = images[0, 0]
    row_count, col_count, _ = pictures.shape
    taps = kernel.shape[1]
    dp, row, grp = lax.axis_size("dp"), lax.axis_size("row"), lax.axis_size("grp")
    nx = row // 2
    hid = w_in.shape[2]
    inv_count = 1.0 / (images.shape[1] * dp * row_count * row * col_count)
    twin = [(i, i ^ 1) for i in range(row)]
    chips = lambda k: [(i, (i + 2 * k) % row) for i in range(row)]

    head, tail, piece, small = prep(images, w_in, w_out, kernel, gain, scale, grp * dp)
    top = lax.ppermute(tail, "row", [(i, i + 1) for i in range(row - 1)])
    bot = lax.ppermute(head, "row", [(i + 1, i) for i in range(row - 1)])
    men_small = lax.ppermute(small, "grp", ring("grp", 1))
    line = lax.all_to_all(piece, ("grp", "dp"), 0, 0, tiled=True)
    hops = [line] + [lax.ppermute(line, "row", chips(k)) for k in range(1, nx)]
    bufs = []
    for block in hops:
        bufs += [block, lax.ppermute(block, "row", twin)]

    filt_a = conv(pictures, top, bot, small, men_small, taps, 0)
    filt_b = conv(pictures, top, bot, small, men_small, taps, 1)
    feat, keep, send = pointwise(
        bufs, filt_a, filt_b, pictures, top, bot, small, men_small, hid, taps, inv_count
    )
    wide = lambda a: a.astype(F32)
    other = lax.ppermute(send, "row", twin)
    chip = (wide(keep) + wide(other)).astype(BF)
    sent = [lax.ppermute(chip[k], "row", chips(k)) for k in range(1, nx)]
    line_sum = wide(chip[0])
    for block in sent:
        line_sum = line_sum + wide(block)
    line_sum = line_sum.astype(BF)
    rest = line_sum[dp * 16 :]
    line_sum = line_sum[: dp * 16].reshape(dp, 16, 256)
    rest = jnp.broadcast_to(rest[None], (dp,) + rest.shape)
    piece_sum = total(lax.all_to_all(jnp.concatenate([line_sum, rest], axis=1), "dp", 0, 0, tiled=True))
    grad_in, grad_out, grad_kern, *rest = finish(spread(piece_sum.astype(BF), "row"), taps)
    return (feat.reshape(images.shape), grad_in, grad_out, grad_kern.transpose(2, 0, 1, 3), *rest)


def solution(mesh):
    in_specs = (
        P("grp", "dp", "row", None, None),
        P("grp", "dp", None),
        P("grp", "dp", None),
        P("grp", None, None, None),
        P("grp", None),
        P("grp", None),
    )
    out_specs = in_specs
    return jax.shard_map(step, mesh=mesh, in_specs=in_specs, out_specs=out_specs, check_vma=False)
```

```python
import functools

import jax
import jax.numpy as jnp
from jax import lax
from jax.experimental import pallas as pl
from jax.experimental.pallas import tpu as pltpu
from jax.sharding import PartitionSpec as P


SQRT_HALF = 0.7071067811865476
INV_SQRT_TAU = 0.3989422804014327
BF = jnp.bfloat16
F32 = jnp.float32
SUB = 512
TILE = 512
LEFT = 8


def ring(axis, shift):
    count = lax.axis_size(axis)
    return [(i, (i + shift) % count) for i in range(count)]


def edges_kernel(images, head, tail, sems):
    rows, edge = images.shape[2], head.shape[0]
    up = pltpu.make_async_copy(images.at[0, 0, pl.ds(0, edge)], head, sems.at[0])
    down = pltpu.make_async_copy(images.at[0, 0, pl.ds(rows - edge, edge)], tail, sems.at[1])
    up.start()
    down.start()
    up.wait()
    down.wait()


def edges(images, edge):
    out = jax.ShapeDtypeStruct((edge,) + images.shape[3:], BF)
    return pl.pallas_call(
        edges_kernel,
        out_shape=[out, out],
        in_specs=[pl.BlockSpec(memory_space=pl.ANY)],
        scratch_shapes=[pltpu.SemaphoreType.DMA((2,))],
        name="edges",
    )(images)


def prep_kernel(w_in, w_out, kernel, gain, scale, piece, small, lines):
    me = lax.axis_index("row")
    me_x, me_c = lax.div(me, 2), lax.rem(me, 2)
    part_in = w_in[0, :, pl.ds(pl.multiple_of(128 * me, 128), 128)]
    part_out = w_out[0, pl.ds(pl.multiple_of(16 * me_x, 16), 16), pl.ds(pl.multiple_of(128 * me_c, 128), 128)]
    for q in range(piece.shape[0]):
        piece[q, :, 0:128] = part_in
        piece[q, :, 128:256] = part_out
    taps = kernel.shape[1]
    lines[...] = jnp.zeros_like(lines)
    for i in range(taps):
        lines[i * taps : i * taps + taps, :] = kernel[0, i].astype(F32)
    lines[taps * taps : taps * taps + 1, :] = gain[...].astype(F32)
    lines[taps * taps + 1 : taps * taps + 2, :] = scale[...].astype(F32)
    small[...] = lines[...].astype(BF)


def prep(w_in, w_out, kernel, gain, scale, copies):
    chans = gain.shape[1]
    return pl.pallas_call(
        prep_kernel,
        out_shape=[
            jax.ShapeDtypeStruct((copies, 16, 256), BF),
            jax.ShapeDtypeStruct((64, chans), BF),
        ],
        scratch_shapes=[pltpu.VMEM((64, chans), F32)],
        name="prep",
    )(w_in, w_out, kernel, gain, scale)


def finish_kernel(done, grad_in, grad_out, grad_kern, grad_gain, grad_scale, lines):
    row = done.shape[0]
    taps = grad_kern.shape[0]
    for r in range(row):
        grad_in[0, :, 128 * r : 128 * r + 128] = done[r, 0:16, 0:128].astype(F32)
        x, h = r // 2, r % 2
        grad_out[0, 16 * x : 16 * x + 16, 128 * h : 128 * h + 128] = done[r, 0:16, 128:256].astype(F32)
        lines[8 * r : 8 * r + 8, :] = done[r, 16:24, :].astype(F32)
    for q in range(taps * taps):
        grad_kern[q // taps, q % taps] = lines[q : q + 1, :]
    grad_gain[...] = lines[taps * taps : taps * taps + 1, :]
    grad_scale[...] = lines[taps * taps + 1 : taps * taps + 2, :]


def finish(done, taps):
    row, _, chans = done.shape
    return pl.pallas_call(
        finish_kernel,
        out_shape=[
            jax.ShapeDtypeStruct((1, 16, 128 * row), F32),
            jax.ShapeDtypeStruct((1, 8 * row, 256), F32),
            jax.ShapeDtypeStruct((taps, taps, 1, chans), F32),
            jax.ShapeDtypeStruct((1, chans), F32),
            jax.ShapeDtypeStruct((1, chans), F32),
        ],
        scratch_shapes=[pltpu.VMEM((8 * row, chans), F32)],
        name="finish",
    )(done)


def fill_padded(pad, img, top, bot, edge):
    rows, cols, chans = img.shape
    zero = jnp.zeros((8, 128), F32)
    for cb in range(chans // 128):
        lanes = slice(cb * 128, cb * 128 + 128)
        for r in range(rows + 2 * edge):
            if r < edge:
                ref, q = top, r
            elif r < rows + edge:
                ref, q = img, r - edge
            else:
                ref, q = bot, r - rows - edge
            pad[cb, r, 0:LEFT, :] = zero
            pad[cb, r, LEFT + cols : LEFT + cols + 8, :] = zero
            pad[cb, r, LEFT : LEFT + cols, :] = ref[q, :, lanes].astype(F32)


def tree(terms):
    while len(terms) > 1:
        terms = [
            terms[a] + terms[a + 1] if a + 1 < len(terms) else terms[a] for a in range(0, len(terms), 2)
        ]
    return terms[0]


def conv_kernel(img, top, bot, own, men, filt, pad, wide_taps, *, taps):
    rows, _, _ = img.shape
    edge = taps // 2
    span = filt.shape[2]
    base = pl.program_id(0) * span

    @pl.when(pl.program_id(0) == 0)
    def _():
        fill_padded(pad, img, top, bot, edge)
        for s, small in ((0, own), (1, men)):
            lines = small[...].astype(F32)
            for q in range(taps * taps):
                wide_taps[s, q] = jnp.broadcast_to(lines[q : q + 1, :], (16, 128)).astype(BF)

    def block(wb, _):
        at = pl.multiple_of(wb * 16, 16)
        w0 = pl.multiple_of(base + at, 16)
        accs = {}
        for j in range(taps):
            vs = [
                pad[0, r, pl.ds(w0 + (LEFT - edge + j), 16), :].astype(BF) for r in range(rows + 2 * edge)
            ]
            for s in range(2):
                w = [wide_taps[s, i * taps + j] for i in range(taps)]
                for h in range(rows):
                    term = tree([vs[h + i] * w[i] for i in range(taps)]).astype(F32)
                    accs[s, h] = term if j == 0 else accs[s, h] + term
        for h in range(rows):
            for s in range(2):
                filt[s, h, pl.ds(at, 16), :] = accs[s, h]
        return 0

    lax.fori_loop(0, span // 16, block, 0)


def conv(img, top, bot, own, men, taps, cb):
    rows, cols, _ = img.shape
    edge = taps // 2
    lanes = lambda a: pl.BlockSpec(a.shape[:-1] + (128,), lambda t: (0,) * (a.ndim - 1) + (cb,))
    return pl.pallas_call(
        functools.partial(conv_kernel, taps=taps),
        out_shape=jax.ShapeDtypeStruct((2, rows, cols, 128), F32),
        grid=(4,),
        in_specs=[lanes(img), lanes(top), lanes(bot), lanes(own), lanes(men)],
        out_specs=pl.BlockSpec((2, rows, cols // 4, 128), lambda t: (0, 0, t, 0)),
        scratch_shapes=[
            pltpu.VMEM((1, rows + 2 * edge, cols + LEFT + 8, 128), F32),
            pltpu.VMEM((2, taps * taps, 16, 128), BF),
        ],
    )(img, top, bot, own, men)


def tap_grad(img, top, bot, up, gsum, pad, lines, taps):
    rows, cols, chans = img.shape
    edge = taps // 2
    fill_padded(pad, img, top, bot, edge)
    lines[...] = jnp.zeros_like(lines)
    for cb in range(chans // 128):
        lanes = slice(cb * 128, cb * 128 + 128)
        for lo, hi in ((0, 4), (4, taps)):

            def block(wb, accs):
                accs = list(accs)
                for u in range(2):
                    w0 = pl.multiple_of(wb * 32 + u * 16, 16)
                    ups = [up[h, pl.ds(w0, 16), lanes] for h in range(rows)]
                    for j in range(lo, hi):
                        vs = [
                            pad[cb, r, pl.ds(w0 + (LEFT - edge + j), 16), :].astype(BF)
                            for r in range(rows + 2 * edge)
                        ]
                        for i in range(taps):
                            term = tree([vs[h + i] * ups[h] for h in range(rows)]).astype(F32)
                            q = (j - lo) * taps + i
                            accs[q] = accs[q] + (term[:8] + term[8:])
                return tuple(accs)

            count = (hi - lo) * taps
            accs = lax.fori_loop(
                0, cols // 32, block, tuple(jnp.zeros((8, 128), F32) for _ in range(count))
            )
            for q in range(count):
                tap = (q % taps) * taps + lo + q // taps
                lines[tap : tap + 1, lanes] = jnp.sum(accs[q], axis=0, keepdims=True)
        for q in range(2):
            lines[taps * taps + q : taps * taps + q + 1, lanes] = gsum[q : q + 1, lanes]


def pointwise_kernel(*refs, nx, taps, inv_count):
    count = taps * taps
    bufs = refs[: 2 * nx]
    (filt_a, filt_b, img, top, bot, own, men) = refs[2 * nx : 2 * nx + 7]
    (feat, keep, send) = refs[2 * nx + 7 : 2 * nx + 10]
    (w_in, w_out, act, slope, g_in, g_out, normed, up_branch, up_pre, unit_s, up_conv, gsum, pad, lines) = refs[2 * nx + 10 :]
    gain = own[count : count + 1, :].astype(F32)
    s_own = own[count + 1 : count + 2, :].astype(F32)
    s_men = men[count + 1 : count + 2, :].astype(F32)
    step = pl.program_id(0)
    _, cols, chans = img.shape
    tile = feat.shape[0]
    hid = w_out.shape[2]
    dp = bufs[0].shape[0] // 2
    chunks = hid // 256
    me, me_g = lax.axis_index("row"), lax.axis_index("grp")
    me_x, me_c = lax.div(me, 2), lax.rem(me, 2)
    per_d = hid // dp

    @pl.when(step == 0)
    def _():
        for k in range(nx):
            x = lax.rem(me_x - k + nx, nx)
            for c in range(2):
                h = me_c if c == 0 else 1 - me_c
                buf = bufs[2 * k + c]
                for d in range(dp):
                    for s in range(2):
                        q = dp * (me_g if s == 0 else 1 - me_g) + d
                        w_in[s, 2 * x + h, d * 16 : d * 16 + 16, :] = buf[q, :, 0:128]
                        at = pl.multiple_of(d * per_d + x * 16, 16)
                        w_out[s, h, pl.ds(at, 16), :] = buf[q, :, 128:256]
        g_in[...] = jnp.zeros_like(g_in)
        g_out[...] = jnp.zeros_like(g_out)
        gsum[...] = jnp.zeros_like(gsum)

    def in_chunk(s, n):
        return jnp.concatenate([w_in[s, 2 * n], w_in[s, 2 * n + 1]], axis=1)

    def out_chunk(s, n):
        rows = slice(n * 256, n * 256 + 256)
        return jnp.concatenate([w_out[s, 0, rows, :], w_out[s, 1, rows, :]], axis=1)

    per_row = max(1, cols // SUB)

    def block(m, _):
        at = pl.multiple_of(m * SUB, SUB)
        line, w0 = (lax.div(m, per_row), pl.multiple_of(lax.rem(m, per_row) * SUB, SUB)) if SUB <= cols else (pl.ds(m * (SUB // cols), SUB // cols), 0)
        here = pl.ds(at, SUB)
        branch = [None, None]
        for s, small in ((0, own), (1, men)):
            x = jnp.concatenate([f[s, line, pl.ds(w0, min(SUB, cols)), :].reshape(SUB, 128) for f in (filt_a, filt_b)], axis=1)
            centred = x - jnp.mean(x, axis=-1, keepdims=True)
            inv = lax.rsqrt(jnp.mean(centred * centred, axis=-1, keepdims=True) + 1e-06)
            x = centred * inv
            if s == 0:
                unit_s[...] = x
                inv_std = inv
            x = (x * small[count : count + 1, :].astype(F32)).astype(BF)
            if s == 0:
                normed[here, :] = x
            for n in range(chunks):
                pre = jnp.dot(x, in_chunk(s, n), preferred_element_type=F32)
                half_cdf = 0.5 + 0.5 * lax.erf(pre * SQRT_HALF)
                activated = (pre * half_cdf).astype(BF)
                if s == 0:
                    act[here, n * 256 : n * 256 + 256] = activated
                    slope[:, n * 256 : n * 256 + 256] = (
                        half_cdf + pre * jnp.exp(-0.5 * pre * pre) * INV_SQRT_TAU
                    )
                part = jnp.dot(activated, out_chunk(s, n), preferred_element_type=F32)
                branch[s] = part if branch[s] is None else branch[s] + part
        scaled = branch[0] * s_own
        feat[here, :] = (img[pl.ds(step * (tile // cols), tile // cols)].reshape(tile, chans).astype(F32) + scaled).astype(BF)
        upstream = (scaled - s_men * branch[1]) * inv_count
        gsum[1:2, :] = gsum[1:2, :] + jnp.sum(upstream * branch[0], axis=0, keepdims=True)
        back = (upstream * s_own).astype(BF)
        up_branch[here, :] = back
        up_normed = None
        for n in range(chunks):
            lanes = slice(n * 256, n * 256 + 256)
            up_active = lax.dot_general(
                back, out_chunk(0, n), (((1,), (1,)), ((), ())), preferred_element_type=F32
            )
            up_p = (up_active * slope[:, lanes]).astype(BF)
            up_pre[here, lanes] = up_p
            part = lax.dot_general(
                up_p, in_chunk(0, n), (((1,), (1,)), ((), ())), preferred_element_type=F32
            )
            up_normed = part if up_normed is None else up_normed + part
        unit = unit_s[...]
        prod = up_normed * unit
        gsum[0:1, :] = gsum[0:1, :] + jnp.sum(prod, axis=0, keepdims=True)
        up_unit = up_normed * gain
        mean_up = jnp.mean(up_unit, axis=-1, keepdims=True)
        mean_proj = jnp.mean(prod * gain, axis=-1, keepdims=True)
        slab = (inv_std * (up_unit - mean_up - unit * mean_proj)).astype(BF)
        up_conv[pl.ds(step * (tile // cols), tile // cols)] = slab.reshape(tile // cols, cols, chans)
        return 0

    lax.fori_loop(0, tile // SUB, block, 0)
    normed_t = normed[...].T
    up_branch_t = up_branch[...].T
    for n in range(chunks):
        lanes = slice(n * 256, n * 256 + 256)
        g_out[:, lanes] = g_out[:, lanes] + jnp.dot(up_branch_t, act[:, lanes], preferred_element_type=F32)
        g_in[:, lanes] = g_in[:, lanes] + jnp.dot(normed_t, up_pre[:, lanes], preferred_element_type=F32)

    @pl.when(step == pl.num_programs(0) - 1)
    def _():
        tap_grad(img, top, bot, up_conv, gsum, pad, lines, taps)
        g_out_t = g_out[...].astype(BF).T
        for x in range(nx):
            for h in range(2):
                xr = lax.rem(x - me_x + nx, nx)
                lanes = slice(128 * (2 * x + h), 128 * (2 * x + h) + 128)

                def emit(out):
                    for d in range(dp):
                        to = slice(d * 16, d * 16 + 16)
                        out[xr, to, 0:128] = g_in[to, lanes].astype(BF)
                        lo = d * per_d + 16 * x
                        out[xr, to, 128:256] = g_out_t[lo : lo + 16, 128 * h : 128 * h + 128]
                    r = 2 * x + h
                    out[xr, dp * 16 : dp * 16 + 8, :] = lines[8 * r : 8 * r + 8, :].astype(BF)

                pl.when(me_c == h)(functools.partial(emit, keep))
                pl.when(me_c != h)(functools.partial(emit, send))


def pointwise(bufs, filt_a, filt_b, img, top, bot, own, men, hid, taps, inv_count):
    rows, cols, chans = img.shape
    pixels = rows * cols
    nx = len(bufs) // 2
    dp = bufs[0].shape[0] // 2
    edge = taps // 2
    tile = TILE
    whole = lambda a: pl.BlockSpec(a.shape, lambda t: (0,) * a.ndim)
    filt = pl.BlockSpec((2, tile // cols, cols, 128), lambda t: (0, t, 0, 0))
    part = pl.BlockSpec((nx, dp * 16 + 8, 256), lambda t: (0, 0, 0))
    return pl.pallas_call(
        functools.partial(pointwise_kernel, nx=nx, taps=taps, inv_count=inv_count),
        out_shape=[
            jax.ShapeDtypeStruct((pixels, chans), BF),
            jax.ShapeDtypeStruct((nx, dp * 16 + 8, 256), BF),
            jax.ShapeDtypeStruct((nx, dp * 16 + 8, 256), BF),
        ],
        grid=(pixels // tile,),
        in_specs=[whole(b) for b in bufs] + [filt, filt] + [whole(a) for a in (img, top, bot, own, men)],
        out_specs=[pl.BlockSpec((tile, chans), lambda t: (t, 0)), part, part],
        scratch_shapes=[
            pltpu.VMEM((2, hid // 128, chans, 128), BF),
            pltpu.VMEM((2, 2, hid, 128), BF),
            pltpu.VMEM((tile, hid), BF),
            pltpu.VMEM((SUB, hid), F32),
            pltpu.VMEM((chans, hid), F32),
            pltpu.VMEM((chans, hid), F32),
            pltpu.VMEM((tile, chans), BF),
            pltpu.VMEM((tile, chans), BF),
            pltpu.VMEM((tile, hid), BF),
            pltpu.VMEM((SUB, chans), F32),
            pltpu.VMEM((rows, cols, chans), BF),
            pltpu.VMEM((8, chans), F32),
            pltpu.VMEM((chans // 128, rows + 2 * edge, cols + LEFT + 8, 128), F32),
            pltpu.VMEM((64, chans), F32),
        ],
        name="pointwise",
    )(*bufs, filt_a, filt_b, img, top, bot, own, men)


def total(block):
    return jnp.sum(block.astype(F32), axis=0)


def spread(block, axis):
    copies = jnp.broadcast_to(block[None], (lax.axis_size(axis),) + block.shape)
    return lax.all_to_all(copies, axis, 0, 0, tiled=True)


def step(images, w_in, w_out, kernel, gain, scale):
    pictures = images[0, 0]
    row_count, col_count, _ = pictures.shape
    taps = kernel.shape[1]
    dp, row, grp = lax.axis_size("dp"), lax.axis_size("row"), lax.axis_size("grp")
    nx = row // 2
    hid = w_in.shape[2]
    inv_count = 1.0 / (images.shape[1] * dp * row_count * row * col_count)
    twin = [(i, i ^ 1) for i in range(row)]
    chips = lambda k: [(i, (i + 2 * k) % row) for i in range(row)]

    piece, small = prep(w_in, w_out, kernel, gain, scale, grp * dp)
    head, tail = edges(images, taps // 2)
    top = lax.ppermute(tail, "row", [(i, i + 1) for i in range(row - 1)])
    bot = lax.ppermute(head, "row", [(i + 1, i) for i in range(row - 1)])
    men_small = lax.ppermute(small, "grp", ring("grp", 1))
    line = lax.all_to_all(piece, ("grp", "dp"), 0, 0, tiled=True)
    hops = [line] + [lax.ppermute(line, "row", chips(k)) for k in range(1, nx)]
    bufs = []
    for block in hops:
        bufs += [block, lax.ppermute(block, "row", twin)]

    filt_a = conv(pictures, top, bot, small, men_small, taps, 0)
    filt_b = conv(pictures, top, bot, small, men_small, taps, 1)
    feat, keep, send = pointwise(
        bufs, filt_a, filt_b, pictures, top, bot, small, men_small, hid, taps, inv_count
    )
    wide = lambda a: a.astype(F32)
    other = lax.ppermute(send, "row", twin)
    chip = (wide(keep) + wide(other)).astype(BF)
    sent = [lax.ppermute(chip[k], "row", chips(k)) for k in range(1, nx)]
    line_sum = wide(chip[0])
    for block in sent:
        line_sum = line_sum + wide(block)
    line_sum = line_sum.astype(BF)
    rest = line_sum[dp * 16 :]
    line_sum = line_sum[: dp * 16].reshape(dp, 16, 256)
    rest = jnp.broadcast_to(rest[None], (dp,) + rest.shape)
    piece_sum = total(lax.all_to_all(jnp.concatenate([line_sum, rest], axis=1), "dp", 0, 0, tiled=True))
    grad_in, grad_out, grad_kern, *rest = finish(spread(piece_sum.astype(BF), "row"), taps)
    return (feat.reshape(images.shape), grad_in, grad_out, grad_kern.transpose(2, 0, 1, 3), *rest)


def solution(mesh):
    in_specs = (
        P("grp", "dp", "row", None, None),
        P("grp", "dp", None),
        P("grp", "dp", None),
        P("grp", None, None, None),
        P("grp", None),
        P("grp", None),
    )
    out_specs = in_specs
    return jax.shard_map(step, mesh=mesh, in_specs=in_specs, out_specs=out_specs, check_vma=False)
```

```python
import functools

import jax
import jax.numpy as jnp
from jax import lax
from jax.experimental import pallas as pl
from jax.experimental.pallas import tpu as pltpu
from jax.sharding import PartitionSpec as P


SQRT_HALF = 0.7071067811865476
INV_SQRT_TAU = 0.3989422804014327
BF = jnp.bfloat16
F32 = jnp.float32
SUB = 1024
TILE = 1024
LEFT = 8


def ring(axis, shift):
    count = lax.axis_size(axis)
    return [(i, (i + shift) % count) for i in range(count)]


def prep_kernel(images, w_in, w_out, kernel, gain, scale, head, tail, piece, small, lines, sems, *, edge):
    rows = images.shape[2]
    up = pltpu.make_async_copy(images.at[0, 0, pl.ds(0, edge)], head, sems.at[0])
    down = pltpu.make_async_copy(images.at[0, 0, pl.ds(rows - edge, edge)], tail, sems.at[1])
    up.start()
    down.start()
    me = lax.axis_index("row")
    me_x, me_c = lax.div(me, 2), lax.rem(me, 2)
    part_in = w_in[0, :, pl.ds(pl.multiple_of(128 * me, 128), 128)]
    part_out = w_out[0, pl.ds(pl.multiple_of(16 * me_x, 16), 16), pl.ds(pl.multiple_of(128 * me_c, 128), 128)]
    for q in range(piece.shape[0]):
        piece[q, :, 0:128] = part_in
        piece[q, :, 128:256] = part_out
    taps = kernel.shape[1]
    lines[...] = jnp.zeros_like(lines)
    for i in range(taps):
        lines[i * taps : i * taps + taps, :] = kernel[0, i].astype(F32)
    lines[taps * taps : taps * taps + 1, :] = gain[...].astype(F32)
    lines[taps * taps + 1 : taps * taps + 2, :] = scale[...].astype(F32)
    small[...] = lines[...].astype(BF)
    up.wait()
    down.wait()


def prep(images, w_in, w_out, kernel, gain, scale, copies):
    cols, chans = images.shape[3:]
    edge = kernel.shape[1] // 2
    anywhere = pl.BlockSpec(memory_space=pl.ANY)
    vmem = pl.BlockSpec(memory_space=pltpu.VMEM)
    return pl.pallas_call(
        functools.partial(prep_kernel, edge=edge),
        out_shape=[
            jax.ShapeDtypeStruct((edge, cols, chans), BF),
            jax.ShapeDtypeStruct((edge, cols, chans), BF),
            jax.ShapeDtypeStruct((copies, 16, 256), BF),
            jax.ShapeDtypeStruct((64, chans), BF),
        ],
        in_specs=[anywhere] + [vmem] * 5,
        out_specs=[vmem] * 4,
        scratch_shapes=[pltpu.VMEM((64, chans), F32), pltpu.SemaphoreType.DMA((2,))],
        name="prep",
    )(images, w_in, w_out, kernel, gain, scale)


def finish_kernel(done, grad_in, grad_out, grad_kern, grad_gain, grad_scale, lines):
    row = done.shape[0]
    taps = grad_kern.shape[0]
    for r in range(row):
        grad_in[0, :, 128 * r : 128 * r + 128] = done[r, 0:16, 0:128].astype(F32)
        x, h = r // 2, r % 2
        grad_out[0, 16 * x : 16 * x + 16, 128 * h : 128 * h + 128] = done[r, 0:16, 128:256].astype(F32)
        lines[8 * r : 8 * r + 8, :] = done[r, 16:24, :].astype(F32)
    for q in range(taps * taps):
        grad_kern[q // taps, q % taps] = lines[q : q + 1, :]
    grad_gain[...] = lines[taps * taps : taps * taps + 1, :]
    grad_scale[...] = lines[taps * taps + 1 : taps * taps + 2, :]


def finish(done, taps):
    row, _, chans = done.shape
    return pl.pallas_call(
        finish_kernel,
        out_shape=[
            jax.ShapeDtypeStruct((1, 16, 128 * row), F32),
            jax.ShapeDtypeStruct((1, 8 * row, 256), F32),
            jax.ShapeDtypeStruct((taps, taps, 1, chans), F32),
            jax.ShapeDtypeStruct((1, chans), F32),
            jax.ShapeDtypeStruct((1, chans), F32),
        ],
        scratch_shapes=[pltpu.VMEM((8 * row, chans), F32)],
        name="finish",
    )(done)


def fill_padded(pad, img, top, bot, edge):
    rows, cols, chans = img.shape
    zero = jnp.zeros((8, 128), F32)
    me = lax.axis_index("row")
    first, last = me == 0, me == lax.axis_size("row") - 1
    for cb in range(chans // 128):
        lanes = slice(cb * 128, cb * 128 + 128)
        for r in range(rows + 2 * edge):
            if r < edge:
                ref, q = top, r
            elif r < rows + edge:
                ref, q = img, r - edge
            else:
                ref, q = bot, r - rows - edge
            pad[cb, r, 0:LEFT, :] = zero
            pad[cb, r, LEFT + cols : LEFT + cols + 8, :] = zero
            line = ref[q, :, lanes].astype(F32)
            if r < edge or r >= rows + edge:
                line = jnp.where(first if r < edge else last, 0.0, line)
            pad[cb, r, LEFT : LEFT + cols, :] = line


def tree(terms):
    while len(terms) > 1:
        terms = [
            terms[a] + terms[a + 1] if a + 1 < len(terms) else terms[a] for a in range(0, len(terms), 2)
        ]
    return terms[0]


def conv_kernel(img, top, bot, own, men, filt, pad, wide_taps, *, taps):
    rows, _, _ = img.shape
    edge = taps // 2
    span = filt.shape[2]
    base = pl.program_id(0) * span

    @pl.when(pl.program_id(0) == 0)
    def _():
        fill_padded(pad, img, top, bot, edge)
        for s, small in ((0, own), (1, men)):
            lines = small[...].astype(F32)
            for q in range(taps * taps):
                wide_taps[s, q] = jnp.broadcast_to(lines[q : q + 1, :], (16, 128)).astype(BF)

    def block(wb, _):
        at = pl.multiple_of(wb * 16, 16)
        w0 = pl.multiple_of(base + at, 16)
        accs = {}
        for j0 in range(0, taps, 2):
            pair = range(j0, min(j0 + 2, taps))
            vs = {
                (j, r): pad[0, r, pl.ds(w0 + (LEFT - edge + j), 16), :].astype(BF)
                for j in pair
                for r in range(rows + 2 * edge)
            }
            for s in range(2):
                w = {(j, i): wide_taps[s, i * taps + j] for j in pair for i in range(taps)}
                for h in range(rows):
                    term = tree([tree([vs[j, h + i] * w[j, i] for i in range(taps)]) for j in pair])
                    term = term.astype(F32)
                    accs[s, h] = term if j0 == 0 else accs[s, h] + term
        for h in range(rows):
            for s in range(2):
                filt[s, h, pl.ds(at, 16), :] = accs[s, h]
        return 0

    lax.fori_loop(0, span // 16, block, 0)


def conv(img, top, bot, own, men, taps, cb):
    rows, cols, _ = img.shape
    edge = taps // 2
    lanes = lambda a: pl.BlockSpec(a.shape[:-1] + (128,), lambda t: (0,) * (a.ndim - 1) + (cb,))
    return pl.pallas_call(
        functools.partial(conv_kernel, taps=taps),
        out_shape=jax.ShapeDtypeStruct((2, rows, cols, 128), F32),
        grid=(4,),
        in_specs=[lanes(img), lanes(top), lanes(bot), lanes(own), lanes(men)],
        out_specs=pl.BlockSpec((2, rows, cols // 4, 128), lambda t: (0, 0, t, 0)),
        scratch_shapes=[
            pltpu.VMEM((1, rows + 2 * edge, cols + LEFT + 8, 128), F32),
            pltpu.VMEM((2, taps * taps, 16, 128), BF),
        ],
    )(img, top, bot, own, men)


def tap_grad(img, top, bot, up, gsum, pad, lines, taps):
    rows, cols, chans = img.shape
    edge = taps // 2
    fill_padded(pad, img, top, bot, edge)
    lines[...] = jnp.zeros_like(lines)
    for cb in range(chans // 128):
        lanes = slice(cb * 128, cb * 128 + 128)
        for lo, hi in ((0, 4), (4, taps)):

            def block(wb, accs):
                accs = list(accs)
                for u in range(2):
                    w0 = pl.multiple_of(wb * 32 + u * 16, 16)
                    ups = [up[h, pl.ds(w0, 16), lanes] for h in range(rows)]
                    for j in range(lo, hi):
                        vs = [
                            pad[cb, r, pl.ds(w0 + (LEFT - edge + j), 16), :].astype(BF)
                            for r in range(rows + 2 * edge)
                        ]
                        for i in range(taps):
                            term = tree([vs[h + i] * ups[h] for h in range(rows)]).astype(F32)
                            q = (j - lo) * taps + i
                            accs[q] = accs[q] + (term[:8] + term[8:])
                return tuple(accs)

            count = (hi - lo) * taps
            accs = lax.fori_loop(
                0, cols // 32, block, tuple(jnp.zeros((8, 128), F32) for _ in range(count))
            )
            for q in range(count):
                tap = (q % taps) * taps + lo + q // taps
                lines[tap : tap + 1, lanes] = jnp.sum(accs[q], axis=0, keepdims=True)
        for q in range(2):
            lines[taps * taps + q : taps * taps + q + 1, lanes] = gsum[q : q + 1, lanes]


def pointwise_kernel(*refs, nx, taps, inv_count):
    count = taps * taps
    bufs = refs[: 2 * nx]
    (filt_a, filt_b, img, top, bot, own, men) = refs[2 * nx : 2 * nx + 7]
    (feat, keep, send) = refs[2 * nx + 7 : 2 * nx + 10]
    (w_in, w_out, act, slope, g_in, g_out, normed, up_branch, up_pre, unit_s, up_conv, gsum, pad, lines) = refs[2 * nx + 10 :]
    gain = own[count : count + 1, :].astype(F32)
    s_own = own[count + 1 : count + 2, :].astype(F32)
    s_men = men[count + 1 : count + 2, :].astype(F32)
    step = pl.program_id(0)
    _, cols, chans = img.shape
    tile = feat.shape[0]
    hid = w_out.shape[2]
    dp = bufs[0].shape[0] // 2
    chunks = hid // 256
    me, me_g = lax.axis_index("row"), lax.axis_index("grp")
    me_x, me_c = lax.div(me, 2), lax.rem(me, 2)
    per_d = hid // dp

    @pl.when(step == 0)
    def _():
        for k in range(nx):
            x = lax.rem(me_x - k + nx, nx)
            for c in range(2):
                h = me_c if c == 0 else 1 - me_c
                buf = bufs[2 * k + c]
                for d in range(dp):
                    for s in range(2):
                        q = dp * (me_g if s == 0 else 1 - me_g) + d
                        w_in[s, 2 * x + h, d * 16 : d * 16 + 16, :] = buf[q, :, 0:128]
                        at = pl.multiple_of(d * per_d + x * 16, 16)
                        w_out[s, h, pl.ds(at, 16), :] = buf[q, :, 128:256]
        g_in[...] = jnp.zeros_like(g_in)
        g_out[...] = jnp.zeros_like(g_out)
        gsum[...] = jnp.zeros_like(gsum)

    def in_chunk(s, n):
        return jnp.concatenate([w_in[s, 2 * n], w_in[s, 2 * n + 1]], axis=1)

    def out_chunk(s, n):
        rows = slice(n * 256, n * 256 + 256)
        return jnp.concatenate([w_out[s, 0, rows, :], w_out[s, 1, rows, :]], axis=1)

    per_row = max(1, cols // SUB)

    def block(m, _):
        at = pl.multiple_of(m * SUB, SUB)
        line, w0 = (lax.div(m, per_row), pl.multiple_of(lax.rem(m, per_row) * SUB, SUB)) if SUB <= cols else (pl.ds(m * (SUB // cols), SUB // cols), 0)
        here = pl.ds(at, SUB)
        branch = [None, None]
        for s, small in ((0, own), (1, men)):
            x = jnp.concatenate([f[s, line, pl.ds(w0, min(SUB, cols)), :].reshape(SUB, 128) for f in (filt_a, filt_b)], axis=1)
            centred = x - jnp.mean(x, axis=-1, keepdims=True)
            inv = lax.rsqrt(jnp.mean(centred * centred, axis=-1, keepdims=True) + 1e-06)
            x = centred * inv
            if s == 0:
                unit_s[...] = x
                inv_std = inv
            x = (x * small[count : count + 1, :].astype(F32)).astype(BF)
            if s == 0:
                normed[here, :] = x
            for n in range(chunks):
                pre = jnp.dot(x, in_chunk(s, n), preferred_element_type=F32)
                half_cdf = 0.5 + 0.5 * lax.erf(pre * SQRT_HALF)
                activated = (pre * half_cdf).astype(BF)
                if s == 0:
                    act[here, n * 256 : n * 256 + 256] = activated
                    slope[:, n * 256 : n * 256 + 256] = (
                        half_cdf + pre * jnp.exp(-0.5 * pre * pre) * INV_SQRT_TAU
                    )
                part = jnp.dot(activated, out_chunk(s, n), preferred_element_type=F32)
                branch[s] = part if branch[s] is None else branch[s] + part
        scaled = branch[0] * s_own
        feat[here, :] = (img[pl.ds(step * (tile // cols), tile // cols)].reshape(tile, chans).astype(F32) + scaled).astype(BF)
        upstream = (scaled - s_men * branch[1]) * inv_count
        gsum[1:2, :] = gsum[1:2, :] + jnp.sum(upstream * branch[0], axis=0, keepdims=True)
        back = (upstream * s_own).astype(BF)
        up_branch[here, :] = back
        up_normed = None
        for n in range(chunks):
            lanes = slice(n * 256, n * 256 + 256)
            up_active = lax.dot_general(
                back, out_chunk(0, n), (((1,), (1,)), ((), ())), preferred_element_type=F32
            )
            up_p = (up_active * slope[:, lanes]).astype(BF)
            up_pre[here, lanes] = up_p
            part = lax.dot_general(
                up_p, in_chunk(0, n), (((1,), (1,)), ((), ())), preferred_element_type=F32
            )
            up_normed = part if up_normed is None else up_normed + part
        unit = unit_s[...]
        prod = up_normed * unit
        gsum[0:1, :] = gsum[0:1, :] + jnp.sum(prod, axis=0, keepdims=True)
        up_unit = up_normed * gain
        mean_up = jnp.mean(up_unit, axis=-1, keepdims=True)
        mean_proj = jnp.mean(prod * gain, axis=-1, keepdims=True)
        slab = (inv_std * (up_unit - mean_up - unit * mean_proj)).astype(BF)
        up_conv[pl.ds(step * (tile // cols), tile // cols)] = slab.reshape(tile // cols, cols, chans)
        return 0

    lax.fori_loop(0, tile // SUB, block, 0)
    normed_t = normed[...].T
    up_branch_t = up_branch[...].T
    for n in range(chunks):
        lanes = slice(n * 256, n * 256 + 256)
        g_out[:, lanes] = g_out[:, lanes] + jnp.dot(up_branch_t, act[:, lanes], preferred_element_type=F32)
        g_in[:, lanes] = g_in[:, lanes] + jnp.dot(normed_t, up_pre[:, lanes], preferred_element_type=F32)

    @pl.when(step == pl.num_programs(0) - 1)
    def _():
        tap_grad(img, top, bot, up_conv, gsum, pad, lines, taps)
        g_out_t = g_out[...].astype(BF).T
        for x in range(nx):
            for h in range(2):
                xr = lax.rem(x - me_x + nx, nx)
                lanes = slice(128 * (2 * x + h), 128 * (2 * x + h) + 128)

                def emit(out):
                    for d in range(dp):
                        to = slice(d * 16, d * 16 + 16)
                        out[xr, to, 0:128] = g_in[to, lanes].astype(BF)
                        lo = d * per_d + 16 * x
                        out[xr, to, 128:256] = g_out_t[lo : lo + 16, 128 * h : 128 * h + 128]
                    r = 2 * x + h
                    out[xr, dp * 16 : dp * 16 + 8, :] = lines[8 * r : 8 * r + 8, :].astype(BF)

                pl.when(me_c == h)(functools.partial(emit, keep))
                pl.when(me_c != h)(functools.partial(emit, send))


def pointwise(bufs, filt_a, filt_b, img, top, bot, own, men, hid, taps, inv_count):
    rows, cols, chans = img.shape
    pixels = rows * cols
    nx = len(bufs) // 2
    dp = bufs[0].shape[0] // 2
    edge = taps // 2
    tile = TILE
    whole = lambda a: pl.BlockSpec(a.shape, lambda t: (0,) * a.ndim)
    filt = pl.BlockSpec((2, tile // cols, cols, 128), lambda t: (0, t, 0, 0))
    part = pl.BlockSpec((nx, dp * 16 + 8, 256), lambda t: (0, 0, 0))
    return pl.pallas_call(
        functools.partial(pointwise_kernel, nx=nx, taps=taps, inv_count=inv_count),
        out_shape=[
            jax.ShapeDtypeStruct((pixels, chans), BF),
            jax.ShapeDtypeStruct((nx, dp * 16 + 8, 256), BF),
            jax.ShapeDtypeStruct((nx, dp * 16 + 8, 256), BF),
        ],
        grid=(pixels // tile,),
        in_specs=[whole(b) for b in bufs] + [filt, filt] + [whole(a) for a in (img, top, bot, own, men)],
        out_specs=[pl.BlockSpec((tile, chans), lambda t: (t, 0)), part, part],
        scratch_shapes=[
            pltpu.VMEM((2, hid // 128, chans, 128), BF),
            pltpu.VMEM((2, 2, hid, 128), BF),
            pltpu.VMEM((tile, hid), BF),
            pltpu.VMEM((SUB, hid), F32),
            pltpu.VMEM((chans, hid), F32),
            pltpu.VMEM((chans, hid), F32),
            pltpu.VMEM((tile, chans), BF),
            pltpu.VMEM((tile, chans), BF),
            pltpu.VMEM((tile, hid), BF),
            pltpu.VMEM((SUB, chans), F32),
            pltpu.VMEM((rows, cols, chans), BF),
            pltpu.VMEM((8, chans), F32),
            pltpu.VMEM((chans // 128, rows + 2 * edge, cols + LEFT + 8, 128), F32),
            pltpu.VMEM((64, chans), F32),
        ],
        name="pointwise",
    )(*bufs, filt_a, filt_b, img, top, bot, own, men)


def total(block):
    return jnp.sum(block.astype(F32), axis=0)


def spread(block, axis):
    copies = jnp.broadcast_to(block[None], (lax.axis_size(axis),) + block.shape)
    return lax.all_to_all(copies, axis, 0, 0, tiled=True)


def step(images, w_in, w_out, kernel, gain, scale):
    pictures = images[0, 0]
    row_count, col_count, _ = pictures.shape
    taps = kernel.shape[1]
    dp, row, grp = lax.axis_size("dp"), lax.axis_size("row"), lax.axis_size("grp")
    nx = row // 2
    hid = w_in.shape[2]
    inv_count = 1.0 / (images.shape[1] * dp * row_count * row * col_count)
    twin = [(i, i ^ 1) for i in range(row)]
    chips = lambda k: [(i, (i + 2 * k) % row) for i in range(row)]

    head, tail, piece, small = prep(images, w_in, w_out, kernel, gain, scale, grp * dp)
    top = lax.ppermute(tail, "row", ring("row", 1))
    bot = lax.ppermute(head, "row", ring("row", -1))
    men_small = lax.ppermute(small, "grp", ring("grp", 1))
    line = lax.all_to_all(piece, ("grp", "dp"), 0, 0, tiled=True)
    hops = [line] + [lax.ppermute(line, "row", chips(k)) for k in range(1, nx)]
    bufs = []
    for block in hops:
        bufs += [block, lax.ppermute(block, "row", twin)]

    filt_a = conv(pictures, top, bot, small, men_small, taps, 0)
    filt_b = conv(pictures, top, bot, small, men_small, taps, 1)
    feat, keep, send = pointwise(
        bufs, filt_a, filt_b, pictures, top, bot, small, men_small, hid, taps, inv_count
    )
    wide = lambda a: a.astype(F32)
    other = lax.ppermute(send, "row", twin)
    chip = (wide(keep) + wide(other)).astype(BF)
    sent = [lax.ppermute(chip[k], "row", chips(k)) for k in range(1, nx)]
    line_sum = wide(chip[0])
    for block in sent:
        line_sum = line_sum + wide(block)
    line_sum = line_sum.astype(BF)
    rest = line_sum[dp * 16 :]
    line_sum = line_sum[: dp * 16].reshape(dp, 16, 256)
    rest = jnp.broadcast_to(rest[None], (dp,) + rest.shape)
    piece_sum = total(lax.all_to_all(jnp.concatenate([line_sum, rest], axis=1), "dp", 0, 0, tiled=True))
    grad_in, grad_out, grad_kern, *rest = finish(spread(piece_sum.astype(BF), "row"), taps)
    return (feat.reshape(images.shape), grad_in, grad_out, grad_kern.transpose(2, 0, 1, 3), *rest)


def solution(mesh):
    in_specs = (
        P("grp", "dp", "row", None, None),
        P("grp", "dp", None),
        P("grp", "dp", None),
        P("grp", None, None, None),
        P("grp", None),
        P("grp", None),
    )
    out_specs = in_specs
    return jax.shard_map(step, mesh=mesh, in_specs=in_specs, out_specs=out_specs, check_vma=False)
```
